128 devices in a mesh: gz: 16 (over z, x_hi, core), gy: 8 (over y, x_lo).
Axes of the slice: x: 4 (x_hi: 2, x_lo: 2; x = x_hi * 2 + x_lo), y: 4, z: 4, core: 2. Of those that a mesh axis runs over, the one named last changes fastest.
Arguments:
- estimate: float32 [512, 256, 512], P('gz', 'gy'), may hold values from 0.5 to 2
- observed: float32 [2, 512, 256, 512], P(None, 'gz', 'gy'), may hold values from 0.2 to 5
- lateral_taps: float32 [2, 2, 15], replicated, may hold values from 0.05 to 1
- axial_taps: float32 [2, 127], replicated, may hold values from 0.05 to 1
Outputs:
- updated: float32 [512, 256, 512], P('gz', 'gy')
The draws below stay inside these ranges and needn't reach their ends.
All inputs are finite; a program needn't handle non-finite values.
Results may differ from the reference program's by a relative error of at most 0.0001.
Values sent between devices are 32-bit elements; how exact they have to be, the bound alone decides.
No kernel may reach another device: no remote copies, remote signals or barrier semaphores. Data moves between devices by JAX's collectives and lax.ppermute only.
A program may use at most 192 MiB of HBM per device.

```python
import math
import jax
import jax.numpy as jnp
from jax import lax

NX = 512
LAT = 15
AX = 127
NZ = 512
NY = 256


def block_levels(own_key, extent, cuts, smallest, high):
    gain, own = 1.0, jax.random.fold_in(own_key, 6)
    for axis_at, blocks in cuts:
        draws = jnp.exp(jax.random.uniform(jax.random.fold_in(own, axis_at), (blocks,), jnp.float32, smallest / len(cuts), high / len(cuts)))
        gain = gain * jnp.repeat(draws, extent[axis_at] // blocks).reshape([-1 if axis == axis_at else 1 for axis in range(len(extent))])
    return gain


def setup_inputs(seed: int = 0) -> dict:
    keys = jax.random.split(jax.random.key(seed), 5)
    return {
        "estimate": jnp.clip(jnp.exp(math.log(2.0) - 1.3862944 * jax.random.uniform(keys[0], (NZ, NY, NX), jnp.float32) ** block_levels(keys[0], (NZ, NY, NX), ((0, 16), (1, 8)), -0.2, 0.2)), 0.5, 2.0),
        "observed": jnp.clip(jnp.exp(math.log(5.0) - 3.218876 * jax.random.uniform(keys[1], (2, NZ, NY, NX), jnp.float32) ** block_levels(keys[1], (2, NZ, NY, NX), ((1, 16), (2, 8)), -0.2, 0.2)), 0.2, 5.0),
        "lateral_taps": jnp.clip(jnp.exp(jax.random.uniform(keys[2], (2, 2, LAT), jnp.float32, math.log(0.05), math.log(1.0))), 0.05, 1.0),
        "axial_taps": jnp.clip(jnp.exp(jax.random.uniform(keys[3], (2, AX), jnp.float32, math.log(0.05), math.log(1.0))), 0.05, 1.0),
    }


def band_matrix(weights, length):
    centre = weights.shape[0] // 2
    row_index = jnp.arange(length, dtype=jnp.int32)[:, None]
    col_index = jnp.arange(length, dtype=jnp.int32)[None, :]
    offset = col_index - row_index + centre
    inside = (offset >= 0) & (offset < weights.shape[0])
    picked = weights[jnp.clip(offset, 0, weights.shape[0] - 1)]
    return jnp.where(inside, picked, jnp.zeros_like(picked))


def along_z(field, matrix):
    return jnp.einsum("ij,jab->iab", matrix, field, precision=lax.Precision.HIGHEST)


def along_y(field, matrix):
    return jnp.einsum("ij,ajb->aib", matrix, field, precision=lax.Precision.HIGHEST)


def along_x(field, matrix):
    return jnp.einsum("abj,ij->abi", field, matrix, precision=lax.Precision.HIGHEST)


def reference(estimate, observed, lateral_taps, axial_taps):
    total = jnp.zeros_like(estimate)
    for view in range(2):
        weight_x = lateral_taps[view, 0] / jnp.sum(lateral_taps[view, 0])
        weight_y = lateral_taps[view, 1] / jnp.sum(lateral_taps[view, 1])
        weight_z = axial_taps[view] / jnp.sum(axial_taps[view])
        band_x = band_matrix(weight_x, estimate.shape[2])
        band_y = band_matrix(weight_y, estimate.shape[1])
        band_z = band_matrix(weight_z, estimate.shape[0])
        blurred = along_z(along_y(along_x(estimate, band_x), band_y), band_z)
        ratio = observed[view] / blurred
        back = along_x(along_y(along_z(ratio, band_z.T), band_y.T), band_x.T)
        total = total + back
    return estimate * (0.5 * total)
```

```python
import jax
import jax.numpy as jnp
from jax import lax
from jax.experimental import pallas as pl
from jax.experimental.pallas import tpu as pltpu
from jax.sharding import PartitionSpec as P

AXES = ("gz", "gy")
F32 = jnp.float32
BF16 = jnp.bfloat16
VMEM_LIMIT = 56 * 1024 * 1024


def device(z, h, c, y, l):
    return ((z * 2 + h) * 2 + c) * 8 + y * 2 + l


def everyone():
    for z in range(4):
        for h in range(2):
            for c in range(2):
                for y in range(4):
                    for l in range(2):
                        yield z, h, c, y, l


def to_block(k):
    pairs = []
    for z, h, c, y, l in everyone():
        target = (2 * h + c) ^ k
        pairs.append((device(z, h, c, y, l), device(z, target >> 1, l, y, target & 1)))
    return pairs


def to_next_z(k):
    pairs = []
    for z, h, c, y, l in everyone():
        other = z - 1 if (h ^ (k >> 1)) == 0 else z + 1
        if 0 <= other < 4:
            pairs.append((device(z, h, c, y, l), device(other, h, c, y, l)))
    return pairs


def to_next_y(step):
    pairs = []
    for z, h, c, y, l in everyone():
        run = 2 * y + c + step
        if 0 <= run < 8:
            pairs.append((device(z, h, c, y, l), device(z, h, run & 1, run >> 1, l)))
    return pairs


def reverse(pairs):
    return [(target, source) for source, target in pairs]


def halves(value):
    high = value.astype(BF16)
    low = (value - high.astype(F32)).astype(BF16)
    return high, low


def mxu(left, right):
    return jnp.dot(left, right, preferred_element_type=F32)


def shape(dims, dtype=F32):
    return jax.ShapeDtypeStruct(dims, dtype)


def whole(dims):
    return pl.BlockSpec(dims, lambda *_: (0,) * len(dims))


SMEM = pl.BlockSpec(memory_space=pltpu.SMEM)
PIECE = (4, 9, 32, 128)
PIECE_BLOCK = pl.BlockSpec((1, 9, 32, 128), lambda g, *_: (g, 0, 0, 0))


def params():
    return pltpu.CompilerParams(vmem_limit_bytes=VMEM_LIMIT)


def cost(flops, count):
    return pl.CostEstimate(flops=flops, bytes_accessed=count, transcendentals=0)


def pack_kernel(column_ref, centre_ref, left_ref, right_ref, out_ref):
    column = column_ref[0]
    lane = lax.broadcasted_iota(jnp.int32, (32, 128), 1)
    take_left = jnp.logical_and(lane >= 120, column > 0)
    take_right = jnp.logical_and(lane < 8, column < 3)
    centre = centre_ref.reshape(256, 128)
    left = left_ref.reshape(256, 128)
    right = right_ref.reshape(256, 128)
    strips = jnp.zeros((32, 128), F32)
    for e in range(8):
        rows = pl.ds(e, 32, stride=8)
        out_ref[0, e] = centre[rows, :]
        edge = jnp.where(take_left, left[rows, :], jnp.where(take_right, right[rows, :], 0.0))
        strips = strips + pltpu.roll(edge, (16 * e + 8) % 128, 1)
    out_ref[0, 8] = strips


def pack(column, estimate):
    block = (32, 8, 128)
    return pl.pallas_call(
        pack_kernel,
        grid_spec=pltpu.PrefetchScalarGridSpec(
            num_scalar_prefetch=1,
            grid=(4,),
            in_specs=[
                pl.BlockSpec(block, lambda g, s: (0, g, s[0])),
                pl.BlockSpec(block, lambda g, s: (0, g, jnp.maximum(s[0] - 1, 0))),
                pl.BlockSpec(block, lambda g, s: (0, g, jnp.minimum(s[0] + 1, 3))),
            ],
            out_specs=PIECE_BLOCK,
        ),
        out_shape=shape(PIECE),
        compiler_params=params(),
        cost_estimate=cost(1 << 20, 3 << 20),
        name="pack",
    )(column, estimate, estimate, estimate)


def turn_kernel(column_ref, in_ref, out_ref):
    rows = in_ref.reshape(256, 128)
    for e in range(8):
        out_ref[0, e] = rows[pl.ds(e, 32, stride=8), :]


def turn(column, observed):
    return pl.pallas_call(
        turn_kernel,
        grid_spec=pltpu.PrefetchScalarGridSpec(
            num_scalar_prefetch=1,
            grid=(2, 4),
            in_specs=[pl.BlockSpec((1, 32, 8, 128), lambda v, g, s: (v, 0, g, s[0]))],
            out_specs=pl.BlockSpec((1, 8, 32, 128), lambda v, g, s: (v, g, 0, 0)),
        ),
        out_shape=shape((2, 32, 32, 128)),
        compiler_params=params(),
        cost_estimate=cost(1 << 20, 3 << 20),
        name="turn",
    )(column, observed)


def weights_kernel(mask_ref, wx_ref, wz_ref, z_ref, zt_ref, x_ref, xth_ref, xtl_ref, full_ref):
    mask = mask_ref[0]
    for v in range(2):
        for part in range(4):
            row = (lax.broadcasted_iota(jnp.int32, (32, 256), 0) + 32 * part) ^ mask
            col = lax.broadcasted_iota(jnp.int32, (32, 256), 1) ^ mask
            tap = (col + 63 - row) & 255

            def pick(t, total, tap=tap, v=v):
                return jnp.where(tap == t, wz_ref[v, t], total)

            full_ref[pl.ds(128 * v + 32 * part, 32), :] = lax.fori_loop(
                0, 127, pick, jnp.zeros((32, 256), F32)
            )
    full = full_ref[...]
    high, low = halves(full)
    z_ref[:, 0:256] = high
    z_ref[:, 256:512] = low
    z_ref[:, 512:768] = high
    high, low = halves(full.T)
    zt_ref[:, 0:256] = high
    zt_ref[:, 256:512] = low
    zt_ref[:, 512:768] = high

    def x_taps(dims, column_dim, v):
        spot = lax.broadcasted_iota(jnp.int32, dims, column_dim)
        own = lax.broadcasted_iota(jnp.int32, dims, 1 - column_dim)
        strip = spot & 15
        column = jnp.where(spot < 128, spot + 8, jnp.where(strip < 8, strip, strip + 128))
        tap = column - own - 1
        total = jnp.zeros(dims, F32)
        for t in range(15):
            total = jnp.where(tap == t, wx_ref[v, t], total)
        return spot, total

    for v in range(2):
        spot, total = x_taps((256, 128), 0, v)
        for e in range(8):
            keep = jnp.logical_or(spot < 128, (spot - 128) // 16 == e)
            high, low = halves(jnp.where(keep, total, 0.0))
            x_ref[v, e, :, 0:128] = high
            x_ref[v, e, :, 128:256] = low
        spot, total = x_taps((128, 256), 1, v)
        for e in range(8):
            keep = jnp.logical_or(spot < 128, (spot - 128) // 16 == e)
            high, low = halves(jnp.where(keep, total, 0.0))
            xth_ref[v, e] = high
            xtl_ref[v, e] = low


def weights(mask, wx, wz):
    outs = [
        shape((256, 768), BF16),
        shape((256, 768), BF16),
        shape((2, 8, 256, 256), BF16),
        shape((2, 8, 128, 256), BF16),
        shape((2, 8, 128, 256), BF16),
    ]
    return pl.pallas_call(
        weights_kernel,
        in_specs=[SMEM, SMEM, SMEM],
        out_specs=[pl.BlockSpec(memory_space=pltpu.VMEM)] * 5,
        out_shape=outs,
        scratch_shapes=[pltpu.VMEM((256, 256), F32)],
        compiler_params=params(),
        cost_estimate=cost(1 << 24, 4 << 20),
        name="weights",
    )(mask, wx, wz)


def forward_kernel(*refs):
    pieces = refs[:8]
    z_ref, x_ref, out_ref = refs[8:]
    z_taps = z_ref[...]

    def along_z(rows):
        lines = [jnp.concatenate([ref[0, row] for ref in pieces], axis=0) for row in rows]
        field = jnp.concatenate(lines, axis=1) if len(lines) > 1 else lines[0]
        high, low = halves(field)
        return mxu(z_taps, jnp.concatenate([high, high, low], axis=0))

    strips = along_z([8])
    strip_halves = [halves(strips[128 * v : 128 * v + 128]) for v in range(2)]
    for pair in range(4):
        both = along_z([2 * pair, 2 * pair + 1])
        for at in range(2):
            e = 2 * pair + at
            for v in range(2):
                high, low = halves(both[128 * v : 128 * v + 128, 128 * at : 128 * at + 128])
                high = jnp.concatenate([high, strip_halves[v][0]], axis=1)
                low = jnp.concatenate([low, strip_halves[v][1]], axis=1)
                first = mxu(high, x_ref[v, e])
                second = mxu(low, x_ref[v, e, :, 0:128])
                out_ref[v, e] = (first[:, 0:128] + first[:, 128:256]) + second


def forward(pieces, z_taps, x_taps):
    return pl.pallas_call(
        forward_kernel,
        grid=(4,),
        in_specs=[PIECE_BLOCK] * 8 + [whole((256, 768)), whole((2, 8, 256, 256))],
        out_specs=pl.BlockSpec((2, 8, 128, 128), lambda g: (0, g, 0, 0)),
        out_shape=shape((2, 32, 128, 128)),
        compiler_params=params(),
        cost_estimate=cost(8 << 30, 16 << 20),
        name="forward",
    )(*pieces, z_taps, x_taps)


def y_sums(wy_ref, low_ref, centre_ref, high_ref, flip, start, store):
    v = pl.program_id(0)
    taps = [wy_ref[v, 14 - t if flip else t] for t in range(15)]

    def line(row):
        if row < 7:
            return low_ref[0, row, pl.ds(start, 8), :]
        if row < 39:
            return centre_ref[0, row - 7, pl.ds(start, 8), :]
        return high_ref[0, row - 39, pl.ds(start, 8), :]

    for y in range(32):
        total = taps[0] * line(y)
        for t in range(1, 15):
            total = total + taps[t] * line(y + t)
        store(y, total)


def ratio_kernel(wy_ref, low_ref, centre_ref, high_ref, *refs):
    observed, out_ref = refs[:4], refs[4]
    for k in range(4):

        @pl.loop(0, 4)
        def _(part, k=k):
            inner = pl.multiple_of(part * 8, 8)
            start = pl.multiple_of(32 * k + part * 8, 8)

            def store(y, total):
                out_ref[0, y, pl.ds(start, 8), :] = observed[k][0, y, pl.ds(inner, 8), :] / total

            y_sums(wy_ref, low_ref, centre_ref, high_ref, False, start, store)


def back_y_kernel(wy_ref, low_ref, centre_ref, high_ref, out_ref):
    @pl.loop(0, 16)
    def _(part):
        start = pl.multiple_of(part * 8, 8)

        def store(y, total):
            out_ref[0, y, pl.ds(start, 8), :] = total

        y_sums(wy_ref, low_ref, centre_ref, high_ref, True, start, store)


def along_y(kernel, name, wy, low, centre, high, extra):
    edge = pl.BlockSpec((1, 7, 128, 128), lambda v: (v, 0, 0, 0))
    middle = pl.BlockSpec((1, 32, 128, 128), lambda v: (v, 0, 0, 0))
    quarter = pl.BlockSpec((1, 32, 32, 128), lambda v: (v, 0, 0, 0))
    return pl.pallas_call(
        kernel,
        grid=(2,),
        in_specs=[SMEM, edge, middle, edge] + [quarter] * len(extra),
        out_specs=middle,
        out_shape=shape((2, 32, 128, 128)),
        compiler_params=params(),
        cost_estimate=cost(30 << 20, 14 << 20),
        name=name,
    )(wy, low, centre, high, *extra)


def backward_kernel(in_ref, xth_ref, xtl_ref, zt_ref, *outs):
    zt_taps = zt_ref[...]

    def along_z(fields, rows):
        high, low = halves(jnp.concatenate(fields, axis=1) if len(fields) > 1 else fields[0])
        result = mxu(zt_taps, jnp.concatenate([high, high, low], axis=0))
        for at, row in enumerate(rows):
            for m in range(8):
                outs[m][0, row] = result[32 * m : 32 * m + 32, 128 * at : 128 * at + 128]

    strips = [jnp.zeros((128, 128), F32), jnp.zeros((128, 128), F32)]
    for pair in range(4):
        fields = []
        for e in (2 * pair, 2 * pair + 1):
            mains = []
            for v in range(2):
                high, low = halves(in_ref[v, e])
                right = xth_ref[v, e]
                wide = mxu(
                    jnp.concatenate([high, low], axis=1), jnp.concatenate([right, right], axis=0)
                ) + mxu(high, xtl_ref[v, e])
                mains.append(wide[:, 0:128])
                strips[v] = strips[v] + wide[:, 128:256]
            fields.append(jnp.concatenate(mains, axis=0))
        along_z(fields, [2 * pair, 2 * pair + 1])
    along_z([jnp.concatenate(strips, axis=0)], [8])


def backward(field, xt_high, xt_low, zt_taps):
    return pl.pallas_call(
        backward_kernel,
        grid=(4,),
        in_specs=[
            pl.BlockSpec((2, 8, 128, 128), lambda g: (0, g, 0, 0)),
            whole((2, 8, 128, 256)),
            whole((2, 8, 128, 256)),
            whole((256, 768)),
        ],
        out_specs=[PIECE_BLOCK] * 8,
        out_shape=[shape(PIECE)] * 8,
        compiler_params=params(),
        cost_estimate=cost(8 << 30, 16 << 20),
        name="backward",
    )(field, xt_high, xt_low, zt_taps)


def finish_kernel(own_ref, p0, p1, p2, p3, estimate_ref, out_ref, all_ref, turn_ref):
    own = own_ref[0]
    for k, ref in enumerate((p0, p1, p2, p3)):
        all_ref[own ^ k] = ref[0]
    lane = lax.broadcasted_iota(jnp.int32, (32, 128), 1)
    ends = jnp.logical_or(lane >= 120, lane < 8)
    from_next = (lane & 8) == 0
    for j in range(4):
        zero = jnp.zeros((32, 128), F32)
        after = all_ref[j + 1, 8] if j < 3 else zero
        before = all_ref[j - 1, 8] if j > 0 else zero
        strips = jnp.where(from_next, after, before)
        for e in range(8):
            moved = pltpu.roll(strips, (120 - 16 * e) % 128, 1)
            turn_ref[pl.ds(e, 32, stride=8), :] = all_ref[j, e] + jnp.where(ends, moved, 0.0)
        columns = pl.ds(128 * j, 128)
        total = turn_ref[...].reshape(32, 8, 128)
        out_ref[:, :, columns] = estimate_ref[:, :, columns] * (0.5 * total)


def finish(own, pieces, estimate):
    slab = pl.BlockSpec((32, 8, 512), lambda g, s: (0, g, 0))
    return pl.pallas_call(
        finish_kernel,
        grid_spec=pltpu.PrefetchScalarGridSpec(
            num_scalar_prefetch=1,
            grid=(4,),
            in_specs=[PIECE_BLOCK] * 4 + [slab],
            out_specs=slab,
            scratch_shapes=[pltpu.VMEM((4, 9, 32, 128), F32), pltpu.VMEM((256, 128), F32)],
        ),
        out_shape=shape((32, 32, 512)),
        compiler_params=params(),
        cost_estimate=cost(2 << 20, 6 << 20),
        name="finish",
    )(own, *pieces, estimate)


def y_edges(field):
    low = lax.ppermute(field[:, 25:32], AXES, to_next_y(1))
    high = lax.ppermute(field[:, 0:7], AXES, to_next_y(-1))
    return low, high


def on_device(estimate, observed, lateral_taps, axial_taps):
    lateral = lateral_taps / jnp.sum(lateral_taps, axis=2, keepdims=True)
    axial = axial_taps / jnp.sum(axial_taps, axis=1, keepdims=True)
    gz, gy = lax.axis_index("gz"), lax.axis_index("gy")
    own = jnp.reshape(gz & 3, (1,))
    mask = jnp.reshape(32 * ((gz & 2) + (gy & 1)), (1,))

    mine = [lax.ppermute(pack(own ^ k, estimate), AXES, to_block(k)) for k in range(4)]
    seen = [lax.ppermute(turn(own ^ k, observed), AXES, to_block(k)) for k in range(4)]
    near = [lax.ppermute(mine[k], AXES, to_next_z(k)) for k in range(4)]
    z_taps, zt_taps, x_taps, xt_high, xt_low = weights(mask, lateral[:, 0], axial)

    blurred = forward(mine + near, z_taps, x_taps)
    low, high = y_edges(blurred)
    ratio = along_y(ratio_kernel, "ratio", lateral[:, 1], low, blurred, high, seen)
    low, high = y_edges(ratio)
    back = along_y(back_y_kernel, "back_y", lateral[:, 1], low, ratio, high, [])
    parts = backward(back, xt_high, xt_low, zt_taps)
    home = []
    for k in range(4):
        added = parts[k] + lax.ppermute(parts[4 + k], AXES, reverse(to_next_z(k)))
        home.append(lax.ppermute(added, AXES, reverse(to_block(k))))
    return finish(own, home, estimate)


def solution(mesh):
    return jax.shard_map(
        on_device,
        mesh=mesh,
        in_specs=(P("gz", "gy", None), P(None, "gz", "gy", None), P(), P()),
        out_specs=P("gz", "gy", None),
        check_vma=False,
    )
```

```python
import jax
import jax.numpy as jnp
from jax import lax
from jax.experimental import pallas as pl
from jax.experimental.pallas import tpu as pltpu
from jax.sharding import PartitionSpec as P

AXES = ("gz", "gy")
F32 = jnp.float32
BF16 = jnp.bfloat16
VMEM_LIMIT = 56 * 1024 * 1024


def device(z, h, c, y, l):
    return ((z * 2 + h) * 2 + c) * 8 + y * 2 + l


def everyone():
    for z in range(4):
        for h in range(2):
            for c in range(2):
                for y in range(4):
                    for l in range(2):
                        yield z, h, c, y, l


def to_block(k):
    pairs = []
    for z, h, c, y, l in everyone():
        target = (2 * h + c) ^ k
        pairs.append((device(z, h, c, y, l), device(z, target >> 1, l, y, target & 1)))
    return pairs


def to_next_z(k):
    pairs = []
    for z, h, c, y, l in everyone():
        other = z - 1 if (h ^ (k >> 1)) == 0 else z + 1
        if 0 <= other < 4:
            pairs.append((device(z, h, c, y, l), device(other, h, c, y, l)))
    return pairs


def to_next_y(step):
    pairs = []
    for z, h, c, y, l in everyone():
        run = 2 * y + c + step
        if 0 <= run < 8:
            pairs.append((device(z, h, c, y, l), device(z, h, run & 1, run >> 1, l)))
    return pairs


def reverse(pairs):
    return [(target, source) for source, target in pairs]


def halves(value):
    high = value.astype(BF16)
    low = (value - high.astype(F32)).astype(BF16)
    return high, low


def mxu(left, right):
    return jnp.dot(left, right, preferred_element_type=F32)


def shape(dims, dtype=F32):
    return jax.ShapeDtypeStruct(dims, dtype)


def whole(dims):
    return pl.BlockSpec(dims, lambda *_: (0,) * len(dims))


SMEM = pl.BlockSpec(memory_space=pltpu.SMEM)
PIECE = (2, 9, 32, 128)
PIECE_BLOCK = pl.BlockSpec((1, 9, 32, 128), lambda g, *_: (g, 0, 0, 0))


def edge_group(g):
    return 3 * g


def inner_group(g):
    return g + 1


EDGE_ROWS = list(range(0, 8)) + list(range(24, 32))
INNER_ROWS = list(range(8, 24))


def params():
    return pltpu.CompilerParams(vmem_limit_bytes=VMEM_LIMIT)


def cost(flops, count):
    return pl.CostEstimate(flops=flops, bytes_accessed=count, transcendentals=0)


def pack_kernel(column_ref, centre_ref, left_ref, right_ref, out_ref):
    column = column_ref[0]
    lane = lax.broadcasted_iota(jnp.int32, (32, 128), 1)
    take_left = jnp.logical_and(lane >= 120, column > 0)
    take_right = jnp.logical_and(lane < 8, column < 3)
    centre = centre_ref.reshape(256, 128)
    left = left_ref.reshape(256, 128)
    right = right_ref.reshape(256, 128)
    strips = jnp.zeros((32, 128), F32)
    for e in range(8):
        rows = pl.ds(e, 32, stride=8)
        out_ref[0, e] = centre[rows, :]
        edge = jnp.where(take_left, left[rows, :], jnp.where(take_right, right[rows, :], 0.0))
        strips = strips + pltpu.roll(edge, (16 * e + 8) % 128, 1)
    out_ref[0, 8] = strips


def pack(group, column, estimate):
    block = (32, 8, 128)
    return pl.pallas_call(
        pack_kernel,
        grid_spec=pltpu.PrefetchScalarGridSpec(
            num_scalar_prefetch=1,
            grid=(2,),
            in_specs=[
                pl.BlockSpec(block, lambda g, s: (0, group(g), s[0])),
                pl.BlockSpec(block, lambda g, s: (0, group(g), jnp.maximum(s[0] - 1, 0))),
                pl.BlockSpec(block, lambda g, s: (0, group(g), jnp.minimum(s[0] + 1, 3))),
            ],
            out_specs=PIECE_BLOCK,
        ),
        out_shape=shape(PIECE),
        compiler_params=params(),
        cost_estimate=cost(1 << 20, 6 << 20),
        name="pack",
    )(column, estimate, estimate, estimate)


def turn_kernel(column_ref, in_ref, out_ref):
    for v in range(2):
        rows = in_ref.at[v].reshape(256, 128)
        for e in range(8):
            out_ref[v, e] = rows[pl.ds(e, 32, stride=8), :]


def turn(group, column, observed):
    return pl.pallas_call(
        turn_kernel,
        grid_spec=pltpu.PrefetchScalarGridSpec(
            num_scalar_prefetch=1,
            grid=(2,),
            in_specs=[pl.BlockSpec((2, 32, 8, 128), lambda g, s: (0, 0, group(g), s[0]))],
            out_specs=pl.BlockSpec((2, 8, 32, 128), lambda g, s: (0, g, 0, 0)),
        ),
        out_shape=shape((2, 16, 32, 128)),
        compiler_params=params(),
        cost_estimate=cost(1 << 20, 6 << 20),
        name="turn",
    )(column, observed)


def weights_kernel(mask_ref, wx_ref, wz_ref, z_ref, zt_ref, x_ref, xth_ref, xtl_ref):
    mask = mask_ref[0]
    row = lax.broadcasted_iota(jnp.int32, (128, 256), 0) ^ mask
    lane = lax.broadcasted_iota(jnp.int32, (128, 256), 1)
    parts = []
    for v in range(2):
        band = jnp.broadcast_to(wz_ref[v : v + 1, :], (128, 256))
        band = pltpu.roll(band, 256 - 63, 1)
        for bit in range(7):
            step = 1 << bit
            band = jnp.where((row & step) != 0, pltpu.roll(band, step, 1), band)
        for step in (32, 64):
            other = jnp.where(
                (lane & step) == 0, pltpu.roll(band, 256 - step, 1), pltpu.roll(band, step, 1)
            )
            band = jnp.where(((lane * 0 + mask) & step) != 0, other, band)
        parts.append(band)
    full = jnp.concatenate(parts, axis=0)
    high, low = halves(full)
    z_ref[:, 0:256] = high
    z_ref[:, 256:512] = low
    z_ref[:, 512:768] = high
    high, low = halves(full.T)
    zt_ref[:, 0:256] = high
    zt_ref[:, 256:512] = low
    zt_ref[:, 512:768] = high

    def x_taps(dims, column_dim, v):
        spot = lax.broadcasted_iota(jnp.int32, dims, column_dim)
        own = lax.broadcasted_iota(jnp.int32, dims, 1 - column_dim)
        strip = spot & 15
        column = jnp.where(spot < 128, spot + 8, jnp.where(strip < 8, strip, strip + 128))
        tap = column - own - 1
        total = jnp.zeros(dims, F32)
        for t in range(15):
            total = jnp.where(tap == t, wx_ref[v, t], total)
        return spot, total

    for v in range(2):
        spot, total = x_taps((256, 128), 0, v)
        for e in range(8):
            keep = jnp.logical_or(spot < 128, (spot - 128) // 16 == e)
            high, low = halves(jnp.where(keep, total, 0.0))
            x_ref[v, e, :, 0:128] = high
            x_ref[v, e, :, 128:256] = low
        spot, total = x_taps((128, 256), 1, v)
        for e in range(8):
            keep = jnp.logical_or(spot < 128, (spot - 128) // 16 == e)
            high, low = halves(jnp.where(keep, total, 0.0))
            xth_ref[v, e] = high
            xtl_ref[v, e] = low


def weights(mask, wx, wz):
    outs = [
        shape((256, 768), BF16),
        shape((256, 768), BF16),
        shape((2, 8, 256, 256), BF16),
        shape((2, 8, 128, 256), BF16),
        shape((2, 8, 128, 256), BF16),
    ]
    return pl.pallas_call(
        weights_kernel,
        in_specs=[SMEM, SMEM, pl.BlockSpec(memory_space=pltpu.VMEM)],
        out_specs=[pl.BlockSpec(memory_space=pltpu.VMEM)] * 5,
        out_shape=outs,
        compiler_params=params(),
        cost_estimate=cost(1 << 24, 16 << 20),
        name="weights",
    )(mask, wx, wz)


def forward_kernel(*refs):
    pieces = refs[:8]
    z_ref, x_ref, out_ref = refs[8:11]
    z_taps = z_ref[...]

    def along_z(rows):
        lines = [jnp.concatenate([ref[0, row] for ref in pieces], axis=0) for row in rows]
        field = jnp.concatenate(lines, axis=1) if len(lines) > 1 else lines[0]
        high, low = halves(field)
        return mxu(z_taps, jnp.concatenate([high, high, low], axis=0))

    strips = along_z([8])
    strip_halves = [halves(strips[128 * v : 128 * v + 128]) for v in range(2)]
    for pair in range(4):
        both = along_z([2 * pair, 2 * pair + 1])
        for at in range(2):
            e = 2 * pair + at
            for v in range(2):
                high, low = halves(both[128 * v : 128 * v + 128, 128 * at : 128 * at + 128])
                high = jnp.concatenate([high, strip_halves[v][0]], axis=1)
                low = jnp.concatenate([low, strip_halves[v][1]], axis=1)
                first = mxu(high, x_ref[v, e])
                second = mxu(low, x_ref[v, e, :, 0:128])
                out_ref[v, e] = (first[:, 0:128] + first[:, 128:256]) + second
    if len(refs) > 11:
        first_ref, last_ref = refs[11:]

        @pl.when(pl.program_id(0) == 0)
        def _():
            first_ref[...] = out_ref[:, 0:7]

        @pl.when(pl.program_id(0) == 1)
        def _():
            last_ref[...] = out_ref[:, 1:8]


def forward(pieces, z_taps, x_taps, edges):
    out_specs = [pl.BlockSpec((2, 8, 128, 128), lambda g: (0, g, 0, 0))]
    out_shape = [shape((2, 16, 128, 128))]
    if edges:
        out_specs += [whole((2, 7, 128, 128))] * 2
        out_shape += [shape((2, 7, 128, 128))] * 2
    return pl.pallas_call(
        forward_kernel,
        grid=(2,),
        in_specs=[PIECE_BLOCK] * 8 + [whole((256, 768)), whole((2, 8, 256, 256))],
        out_specs=out_specs,
        out_shape=out_shape,
        compiler_params=params(),
        cost_estimate=cost(4 << 30, 12 << 20),
        name="forward",
    )(*pieces, z_taps, x_taps)


def y_kernel(rows, flip, with_edges, with_ratio):
    def kernel(wy_ref, edge_ref, inner_ref, *refs):
        refs = list(refs)
        low_ref, high_ref = (refs.pop(0), refs.pop(0)) if with_edges else (None, None)
        observed = [refs.pop(0) for _ in range(4)] if with_ratio else []
        out_ref = refs.pop(0)
        v = pl.program_id(0)
        taps = [wy_ref[v, 14 - t if flip else t] for t in range(15)]

        def sums(start, store):
            def line(row):
                part = pl.ds(start, 8)
                if row < 0:
                    return low_ref[0, row + 7, part, :]
                if row < 8:
                    return edge_ref[0, row, part, :]
                if row < 24:
                    return inner_ref[0, row - 8, part, :]
                if row < 32:
                    return edge_ref[0, row - 16, part, :]
                return high_ref[0, row - 32, part, :]

            for at, row in enumerate(rows):
                total = taps[0] * line(row - 7)
                for t in range(1, 15):
                    total = total + taps[t] * line(row + t - 7)
                store(at, row, total)

        if not with_ratio:

            @pl.loop(0, 16)
            def _(part):
                start = pl.multiple_of(part * 8, 8)

                def store(at, row, total):
                    out_ref[0, at, pl.ds(start, 8), :] = total

                sums(start, store)

            return

        for k in range(4):

            @pl.loop(0, 4)
            def _(part, k=k):
                inner = pl.multiple_of(part * 8, 8)
                start = pl.multiple_of(32 * k + part * 8, 8)

                def store(at, row, total):
                    ratio = observed[k][0, at, pl.ds(inner, 8), :] / total
                    out_ref[0, at, pl.ds(start, 8), :] = ratio
                    if with_edges and row < 7:
                        refs[0][0, row, pl.ds(start, 8), :] = ratio
                    if with_edges and row > 24:
                        refs[1][0, row - 25, pl.ds(start, 8), :] = ratio

                sums(start, store)

    return kernel


def along_y(name, rows, flip, wy, edge, inner, outer, observed):
    seven = pl.BlockSpec((1, 7, 128, 128), lambda v: (v, 0, 0, 0))
    chunk = pl.BlockSpec((1, 16, 128, 128), lambda v: (v, 0, 0, 0))
    quarter = pl.BlockSpec((1, 16, 32, 128), lambda v: (v, 0, 0, 0))
    gives_edges = len(outer) > 0 and len(observed) > 0
    return pl.pallas_call(
        y_kernel(rows, flip, len(outer) > 0, len(observed) > 0),
        grid=(2,),
        in_specs=[SMEM, chunk, chunk] + [seven] * len(outer) + [quarter] * len(observed),
        out_specs=[chunk] + [seven] * (2 * gives_edges),
        out_shape=[shape((2, 16, 128, 128))] + [shape((2, 7, 128, 128))] * (2 * gives_edges),
        compiler_params=params(),
        cost_estimate=cost(15 << 20, 12 << 20),
        name=name,
    )(wy, edge, inner, *outer, *observed)


def backward_kernel(in_ref, xth_ref, xtl_ref, zt_ref, *outs):
    zt_taps = zt_ref[...]

    def along_z(fields, rows):
        high, low = halves(jnp.concatenate(fields, axis=1) if len(fields) > 1 else fields[0])
        result = mxu(zt_taps, jnp.concatenate([high, high, low], axis=0))
        for at, row in enumerate(rows):
            for m in range(8):
                part = result[32 * m : 32 * m + 32, 128 * at : 128 * at + 128]
                if m < 4:
                    outs[m][0, row] = part
                else:
                    outs[4 + (m - 4) // 2][m % 2, 0, row] = part

    strips = [jnp.zeros((128, 128), F32), jnp.zeros((128, 128), F32)]
    for pair in range(4):
        fields = []
        for e in (2 * pair, 2 * pair + 1):
            mains = []
            for v in range(2):
                high, low = halves(in_ref[v, e])
                right = xth_ref[v, e]
                wide = mxu(
                    jnp.concatenate([high, low], axis=1), jnp.concatenate([right, right], axis=0)
                ) + mxu(high, xtl_ref[v, e])
                mains.append(wide[:, 0:128])
                strips[v] = strips[v] + wide[:, 128:256]
            fields.append(jnp.concatenate(mains, axis=0))
        along_z(fields, [2 * pair, 2 * pair + 1])
    along_z([jnp.concatenate(strips, axis=0)], [8])


def backward(field, xt_high, xt_low, zt_taps):
    return pl.pallas_call(
        backward_kernel,
        grid=(2,),
        in_specs=[
            pl.BlockSpec((2, 8, 128, 128), lambda g: (0, g, 0, 0)),
            whole((2, 8, 128, 256)),
            whole((2, 8, 128, 256)),
            whole((256, 768)),
        ],
        out_specs=[PIECE_BLOCK] * 4
        + [pl.BlockSpec((2, 1, 9, 32, 128), lambda g: (0, g, 0, 0, 0))] * 2,
        out_shape=[shape(PIECE)] * 4 + [shape((2,) + PIECE)] * 2,
        compiler_params=params(),
        cost_estimate=cost(4 << 30, 12 << 20),
        name="backward",
    )(field, xt_high, xt_low, zt_taps)


def finish_kernel(own_ref, p0, p1, p2, p3, estimate_ref, *refs):
    out_ref, all_ref, turn_ref = refs[-3:]
    own = own_ref[0]
    for k, ref in enumerate((p0, p1, p2, p3)):
        all_ref[own ^ k] = ref[0]
    lane = lax.broadcasted_iota(jnp.int32, (32, 128), 1)
    ends = jnp.logical_or(lane >= 120, lane < 8)
    from_next = (lane & 8) == 0
    for j in range(4):
        zero = jnp.zeros((32, 128), F32)
        after = all_ref[j + 1, 8] if j < 3 else zero
        before = all_ref[j - 1, 8] if j > 0 else zero
        strips = jnp.where(from_next, after, before)
        for e in range(8):
            moved = pltpu.roll(strips, (120 - 16 * e) % 128, 1)
            turn_ref[pl.ds(e, 32, stride=8), :] = all_ref[j, e] + jnp.where(ends, moved, 0.0)
        columns = pl.ds(128 * j, 128)
        total = turn_ref[...].reshape(32, 8, 128)
        out_ref[:, :, columns] = estimate_ref[:, :, columns] * (0.5 * total)


def finish(group, own, pieces, estimate, partial):
    slab = pl.BlockSpec((32, 8, 512), lambda g, s: (0, group(g), 0))
    more = [] if partial is None else [partial]
    return pl.pallas_call(
        finish_kernel,
        grid_spec=pltpu.PrefetchScalarGridSpec(
            num_scalar_prefetch=1,
            grid=(2,),
            in_specs=[PIECE_BLOCK] * 4 + [slab] + [pl.BlockSpec(memory_space=pl.ANY)] * len(more),
            out_specs=slab,
            scratch_shapes=[pltpu.VMEM((4, 9, 32, 128), F32), pltpu.VMEM((256, 128), F32)],
        ),
        out_shape=shape((32, 32, 512)),
        input_output_aliases={6: 0} if more else {},
        compiler_params=params(),
        cost_estimate=cost(2 << 20, 6 << 20),
        name="finish",
    )(own, *pieces, estimate, *more)


def send(value, pairs):
    return lax.ppermute(value, AXES, pairs)


def on_device(estimate, observed, lateral_taps, axial_taps):
    lateral = lateral_taps / jnp.sum(lateral_taps, axis=2, keepdims=True)
    axial = axial_taps / jnp.sum(axial_taps, axis=1, keepdims=True)
    axial = jnp.pad(axial, ((0, 0), (0, 129)))
    wy = lateral[:, 1]
    gz, gy = lax.axis_index("gz"), lax.axis_index("gy")
    own = jnp.reshape(gz & 3, (1,))
    mask = jnp.reshape(32 * ((gz & 2) + (gy & 1)), (1,))

    mine_e = [send(pack(edge_group, own ^ k, estimate), to_block(k)) for k in range(4)]
    mine_i = [send(pack(inner_group, own ^ k, estimate), to_block(k)) for k in range(4)]
    seen_i = [send(turn(inner_group, own ^ k, observed), to_block(k)) for k in range(4)]
    seen_e = [send(turn(edge_group, own ^ k, observed), to_block(k)) for k in range(4)]
    near_e = [send(mine_e[k], to_next_z(k)) for k in range(4)]
    near_i = [send(mine_i[k], to_next_z(k)) for k in range(4)]
    z_taps, zt_taps, x_taps, xt_high, xt_low = weights(mask, lateral[:, 0], axial)

    blur_e, first, last = forward(mine_e + near_e, z_taps, x_taps, True)
    low, high = send(last, to_next_y(1)), send(first, to_next_y(-1))
    (blur_i,) = forward(mine_i + near_i, z_taps, x_taps, False)
    (ratio_i,) = along_y("ratio_i", INNER_ROWS, False, wy, blur_e, blur_i, [], seen_i)
    ratio_e, first, last = along_y(
        "ratio_e", EDGE_ROWS, False, wy, blur_e, blur_i, [low, high], seen_e
    )
    low, high = send(last, to_next_y(1)), send(first, to_next_y(-1))
    (back_i,) = along_y("back_i", INNER_ROWS, True, wy, ratio_e, ratio_i, [], [])
    parts_i = backward(back_i, xt_high, xt_low, zt_taps)
    (back_e,) = along_y("back_e", EDGE_ROWS, True, wy, ratio_e, ratio_i, [low, high], [])
    parts_e = backward(back_e, xt_high, xt_low, zt_taps)
    result = None
    for group, parts in ((inner_group, parts_i), (edge_group, parts_e)):
        outer = [send(parts[4 + pair], reverse(to_next_z(2 * pair))) for pair in range(2)]
        home = [
            send(parts[k] + outer[k // 2][k % 2], reverse(to_block(k))) for k in range(4)
        ]
        result = finish(group, own, home, estimate, result)
    return result


def solution(mesh):
    return jax.shard_map(
        on_device,
        mesh=mesh,
        in_specs=(P("gz", "gy", None), P(None, "gz", "gy", None), P(), P()),
        out_specs=P("gz", "gy", None),
        check_vma=False,
    )
```

```python
import jax
import jax.numpy as jnp
from jax import lax
from jax.experimental import pallas as pl
from jax.experimental.pallas import tpu as pltpu
from jax.sharding import PartitionSpec as P

AXES = ("gz", "gy")
F32 = jnp.float32
BF16 = jnp.bfloat16
VMEM_LIMIT = 24 * 1024 * 1024


def device(z, h, c, y, l):
    return ((z * 2 + h) * 2 + c) * 8 + y * 2 + l


def everyone():
    for z in range(4):
        for h in range(2):
            for c in range(2):
                for y in range(4):
                    for l in range(2):
                        yield z, h, c, y, l


def to_block(k):
    pairs = []
    for z, h, c, y, l in everyone():
        target = (2 * h + c) ^ k
        pairs.append((device(z, h, c, y, l), device(z, target >> 1, l, y, target & 1)))
    return pairs


def to_next_z(k):
    pairs = []
    for z, h, c, y, l in everyone():
        other = z - 1 if (h ^ (k >> 1)) == 0 else z + 1
        if 0 <= other < 4:
            pairs.append((device(z, h, c, y, l), device(other, h, c, y, l)))
    return pairs


def to_next_y(step):
    pairs = []
    for z, h, c, y, l in everyone():
        run = 2 * y + c + step
        if 0 <= run < 8:
            pairs.append((device(z, h, c, y, l), device(z, h, run & 1, run >> 1, l)))
    return pairs


def reverse(pairs):
    return [(target, source) for source, target in pairs]


def halves(value):
    high = value.astype(BF16)
    low = (value - high.astype(F32)).astype(BF16)
    return high, low


def mxu(left, right):
    return jnp.dot(left, right, preferred_element_type=F32)


def shape(dims, dtype=F32):
    return jax.ShapeDtypeStruct(dims, dtype)


def whole(dims):
    return pl.BlockSpec(dims, lambda *_: (0,) * len(dims))


SMEM = pl.BlockSpec(memory_space=pltpu.SMEM)
PIECE = (2, 9, 32, 128)
WHOLE_PIECE = (4, 9, 32, 128)
PIECE_BLOCK = pl.BlockSpec((1, 9, 32, 128), lambda g, *_: (g, 0, 0, 0))


def edge_group(g):
    return 3 * g


def inner_group(g):
    return g + 1


ORDER = (2, 0, 3, 1)
EDGE_ROWS = list(range(0, 8)) + list(range(24, 32))
INNER_ROWS = list(range(8, 24))


def params():
    return pltpu.CompilerParams(vmem_limit_bytes=VMEM_LIMIT)


def cost(flops, count):
    return pl.CostEstimate(flops=flops, bytes_accessed=count, transcendentals=0)


def pack_kernel(column_ref, centre_ref, left_ref, right_ref, out_ref):
    column = column_ref[0]
    lane = lax.broadcasted_iota(jnp.int32, (32, 128), 1)
    take_left = jnp.logical_and(lane >= 120, column > 0)
    take_right = jnp.logical_and(lane < 8, column < 3)
    centre = centre_ref.reshape(256, 128)
    left = left_ref.reshape(256, 128)
    right = right_ref.reshape(256, 128)
    strips = jnp.zeros((32, 128), F32)
    for e in range(8):
        rows = pl.ds(e, 32, stride=8)
        out_ref[0, e] = centre[rows, :]
        edge = jnp.where(take_left, left[rows, :], jnp.where(take_right, right[rows, :], 0.0))
        strips = strips + pltpu.roll(edge, (16 * e + 8) % 128, 1)
    out_ref[0, 8] = strips


def pack(column, estimate):
    block = (32, 8, 128)
    return pl.pallas_call(
        pack_kernel,
        grid_spec=pltpu.PrefetchScalarGridSpec(
            num_scalar_prefetch=1,
            grid=(4,),
            in_specs=[
                pl.BlockSpec(block, lambda g, s: (0, g, s[0])),
                pl.BlockSpec(block, lambda g, s: (0, g, jnp.maximum(s[0] - 1, 0))),
                pl.BlockSpec(block, lambda g, s: (0, g, jnp.minimum(s[0] + 1, 3))),
            ],
            out_specs=PIECE_BLOCK,
        ),
        out_shape=shape(WHOLE_PIECE),
        compiler_params=params(),
        cost_estimate=cost(1 << 20, 12 << 20),
        name="pack",
    )(column, estimate, estimate, estimate)


def turn_kernel(column_ref, in_ref, out_ref):
    for v in range(2):
        rows = in_ref.at[v].reshape(256, 128)
        for e in range(8):
            out_ref[v, e] = rows[pl.ds(e, 32, stride=8), :]


def turn(column, observed):
    return pl.pallas_call(
        turn_kernel,
        grid_spec=pltpu.PrefetchScalarGridSpec(
            num_scalar_prefetch=1,
            grid=(4,),
            in_specs=[pl.BlockSpec((2, 32, 8, 128), lambda g, s: (0, 0, g, s[0]))],
            out_specs=pl.BlockSpec((2, 8, 32, 128), lambda g, s: (0, g, 0, 0)),
        ),
        out_shape=shape((2, 32, 32, 128)),
        compiler_params=params(),
        cost_estimate=cost(1 << 20, 6 << 20),
        name="turn",
    )(column, observed)


def weights_kernel(mask_ref, wx_ref, wz_ref, z_ref, zt_ref, x_ref, xth_ref, xtl_ref):
    mask = mask_ref[0]
    row = lax.broadcasted_iota(jnp.int32, (128, 256), 0) ^ mask
    lane = lax.broadcasted_iota(jnp.int32, (128, 256), 1)
    parts = []
    for v in range(2):
        band = jnp.broadcast_to(wz_ref[v : v + 1, :], (128, 256))
        band = pltpu.roll(band, 256 - 63, 1)
        for bit in range(7):
            step = 1 << bit
            band = jnp.where((row & step) != 0, pltpu.roll(band, step, 1), band)
        for step in (32, 64):
            other = jnp.where(
                (lane & step) == 0, pltpu.roll(band, 256 - step, 1), pltpu.roll(band, step, 1)
            )
            band = jnp.where(((lane * 0 + mask) & step) != 0, other, band)
        parts.append(band)
    full = jnp.concatenate(parts, axis=0)
    high, low = halves(full)
    z_ref[:, 0:256] = high
    z_ref[:, 256:512] = low
    z_ref[:, 512:768] = high
    high, low = halves(full.T)
    zt_ref[:, 0:256] = high
    zt_ref[:, 256:512] = low
    zt_ref[:, 512:768] = high

    def x_taps(dims, column_dim, v):
        spot = lax.broadcasted_iota(jnp.int32, dims, column_dim)
        own = lax.broadcasted_iota(jnp.int32, dims, 1 - column_dim)
        strip = spot & 15
        column = jnp.where(spot < 128, spot + 8, jnp.where(strip < 8, strip, strip + 128))
        tap = column - own - 1
        total = jnp.zeros(dims, F32)
        for t in range(15):
            total = jnp.where(tap == t, wx_ref[v, t], total)
        return spot, total

    for v in range(2):
        spot, total = x_taps((256, 128), 0, v)
        for e in range(8):
            keep = jnp.logical_or(spot < 128, (spot - 128) // 16 == e)
            high, low = halves(jnp.where(keep, total, 0.0))
            x_ref[v, e, :, 0:128] = high
            x_ref[v, e, :, 128:256] = low
        spot, total = x_taps((128, 256), 1, v)
        for e in range(8):
            keep = jnp.logical_or(spot < 128, (spot - 128) // 16 == e)
            high, low = halves(jnp.where(keep, total, 0.0))
            xth_ref[v, e] = high
            xtl_ref[v, e] = low


def weights(mask, wx, wz):
    outs = [
        shape((256, 768), BF16),
        shape((256, 768), BF16),
        shape((2, 8, 256, 256), BF16),
        shape((2, 8, 128, 256), BF16),
        shape((2, 8, 128, 256), BF16),
    ]
    return pl.pallas_call(
        weights_kernel,
        in_specs=[SMEM, SMEM, pl.BlockSpec(memory_space=pltpu.VMEM)],
        out_specs=[pl.BlockSpec(memory_space=pltpu.VMEM)] * 5,
        out_shape=outs,
        compiler_params=params(),
        cost_estimate=cost(1 << 24, 16 << 20),
        name="weights",
    )(mask, wx, wz)


def forward_kernel(*refs):
    pieces = refs[:8]
    z_ref, x_ref, out_ref = refs[8:11]
    z_taps = z_ref[...]

    def along_z(rows):
        lines = [jnp.concatenate([ref[0, row] for ref in pieces], axis=0) for row in rows]
        field = jnp.concatenate(lines, axis=1) if len(lines) > 1 else lines[0]
        high, low = halves(field)
        return mxu(z_taps, jnp.concatenate([high, high, low], axis=0))

    strips = along_z([8])
    strip_halves = [halves(strips[128 * v : 128 * v + 128]) for v in range(2)]
    for pair in range(4):
        both = along_z([2 * pair, 2 * pair + 1])
        for at in range(2):
            e = 2 * pair + at
            for v in range(2):
                high, low = halves(both[128 * v : 128 * v + 128, 128 * at : 128 * at + 128])
                high = jnp.concatenate([high, strip_halves[v][0]], axis=1)
                low = jnp.concatenate([low, strip_halves[v][1]], axis=1)
                first = mxu(high, x_ref[v, e])
                second = mxu(low, x_ref[v, e, :, 0:128])
                out_ref[v, e] = (first[:, 0:128] + first[:, 128:256]) + second
    if len(refs) > 11:
        first_ref, last_ref = refs[11:]

        @pl.when(pl.program_id(0) == 0)
        def _():
            first_ref[...] = out_ref[:, 0:7]

        @pl.when(pl.program_id(0) == 1)
        def _():
            last_ref[...] = out_ref[:, 1:8]


def forward(group, pieces, z_taps, x_taps, edges):
    out_specs = [pl.BlockSpec((2, 8, 128, 128), lambda g: (0, g, 0, 0))]
    out_shape = [shape((2, 16, 128, 128))]
    if edges:
        out_specs += [whole((2, 7, 128, 128))] * 2
        out_shape += [shape((2, 7, 128, 128))] * 2
    return pl.pallas_call(
        forward_kernel,
        grid=(2,),
        in_specs=[pl.BlockSpec((1, 9, 32, 128), lambda g: (group(g), 0, 0, 0))] * 8
        + [whole((256, 768)), whole((2, 8, 256, 256))],
        out_specs=out_specs,
        out_shape=out_shape,
        compiler_params=params(),
        cost_estimate=cost(4 << 30, 12 << 20),
        name="forward",
    )(*pieces, z_taps, x_taps)


def y_kernel(rows, flip, with_edges, with_ratio):
    def kernel(wy_ref, edge_ref, inner_ref, *refs):
        refs = list(refs)
        low_ref, high_ref = (refs.pop(0), refs.pop(0)) if with_edges else (None, None)
        observed = [refs.pop(0) for _ in range(4)] if with_ratio else []
        out_ref = refs.pop(0)
        v = pl.program_id(0)
        taps = [wy_ref[v, 14 - t if flip else t] for t in range(15)]

        def sums(start, store):
            def line(row):
                part = pl.ds(start, 8)
                if row < 0:
                    return low_ref[0, row + 7, part, :]
                if row < 8:
                    return edge_ref[0, row, part, :]
                if row < 24:
                    return inner_ref[0, row - 8, part, :]
                if row < 32:
                    return edge_ref[0, row - 16, part, :]
                return high_ref[0, row - 32, part, :]

            for at, row in enumerate(rows):
                total = taps[0] * line(row - 7)
                for t in range(1, 15):
                    total = total + taps[t] * line(row + t - 7)
                store(at, row, total)

        if not with_ratio:

            @pl.loop(0, 16)
            def _(part):
                start = pl.multiple_of(part * 8, 8)

                def store(at, row, total):
                    out_ref[0, at, pl.ds(start, 8), :] = total

                sums(start, store)

            return

        for k in range(4):

            @pl.loop(0, 4)
            def _(part, k=k):
                inner = pl.multiple_of(part * 8, 8)
                start = pl.multiple_of(32 * k + part * 8, 8)

                def store(at, row, total):
                    ratio = observed[k][0, row, pl.ds(inner, 8), :] / total
                    out_ref[0, at, pl.ds(start, 8), :] = ratio
                    if with_edges and row < 7:
                        refs[0][0, row, pl.ds(start, 8), :] = ratio
                    if with_edges and row > 24:
                        refs[1][0, row - 25, pl.ds(start, 8), :] = ratio

                sums(start, store)

    return kernel


def along_y(name, rows, flip, wy, edge, inner, outer, observed):
    seven = pl.BlockSpec((1, 7, 128, 128), lambda v: (v, 0, 0, 0))
    chunk = pl.BlockSpec((1, 16, 128, 128), lambda v: (v, 0, 0, 0))
    quarter = pl.BlockSpec((1, 32, 32, 128), lambda v: (v, 0, 0, 0))
    gives_edges = len(outer) > 0 and len(observed) > 0
    return pl.pallas_call(
        y_kernel(rows, flip, len(outer) > 0, len(observed) > 0),
        grid=(2,),
        in_specs=[SMEM, chunk, chunk] + [seven] * len(outer) + [quarter] * len(observed),
        out_specs=[chunk] + [seven] * (2 * gives_edges),
        out_shape=[shape((2, 16, 128, 128))] + [shape((2, 7, 128, 128))] * (2 * gives_edges),
        compiler_params=params(),
        cost_estimate=cost(15 << 20, 12 << 20),
        name=name,
    )(wy, edge, inner, *outer, *observed)


def backward_kernel(in_ref, xth_ref, xtl_ref, zt_ref, *outs):
    zt_taps = zt_ref[...]

    def along_z(fields, rows):
        high, low = halves(jnp.concatenate(fields, axis=1) if len(fields) > 1 else fields[0])
        result = mxu(zt_taps, jnp.concatenate([high, high, low], axis=0))
        for at, row in enumerate(rows):
            for m in range(8):
                part = result[32 * m : 32 * m + 32, 128 * at : 128 * at + 128]
                if m < 4:
                    outs[m][0, row] = part
                else:
                    outs[4 + (m - 4) // 2][m % 2, 0, row] = part

    strips = [jnp.zeros((128, 128), F32), jnp.zeros((128, 128), F32)]
    for pair in range(4):
        fields = []
        for e in (2 * pair, 2 * pair + 1):
            mains = []
            for v in range(2):
                high, low = halves(in_ref[v, e])
                right = xth_ref[v, e]
                wide = mxu(
                    jnp.concatenate([high, low], axis=1), jnp.concatenate([right, right], axis=0)
                ) + mxu(high, xtl_ref[v, e])
                mains.append(wide[:, 0:128])
                strips[v] = strips[v] + wide[:, 128:256]
            fields.append(jnp.concatenate(mains, axis=0))
        along_z(fields, [2 * pair, 2 * pair + 1])
    along_z([jnp.concatenate(strips, axis=0)], [8])


def backward(field, xt_high, xt_low, zt_taps):
    return pl.pallas_call(
        backward_kernel,
        grid=(2,),
        in_specs=[
            pl.BlockSpec((2, 8, 128, 128), lambda g: (0, g, 0, 0)),
            whole((2, 8, 128, 256)),
            whole((2, 8, 128, 256)),
            whole((256, 768)),
        ],
        out_specs=[PIECE_BLOCK] * 4
        + [pl.BlockSpec((2, 1, 9, 32, 128), lambda g: (0, g, 0, 0, 0))] * 2,
        out_shape=[shape(PIECE)] * 4 + [shape((2,) + PIECE)] * 2,
        compiler_params=params(),
        cost_estimate=cost(4 << 30, 12 << 20),
        name="backward",
    )(field, xt_high, xt_low, zt_taps)


def finish_kernel(own_ref, p0, p1, p2, p3, estimate_ref, *refs):
    out_ref, all_ref, turn_ref = refs[-3:]
    own = own_ref[0]
    for k, ref in enumerate((p0, p1, p2, p3)):
        all_ref[own ^ k] = ref[0]
    lane = lax.broadcasted_iota(jnp.int32, (32, 128), 1)
    ends = jnp.logical_or(lane >= 120, lane < 8)
    from_next = (lane & 8) == 0
    for j in range(4):
        zero = jnp.zeros((32, 128), F32)
        after = all_ref[j + 1, 8] if j < 3 else zero
        before = all_ref[j - 1, 8] if j > 0 else zero
        strips = jnp.where(from_next, after, before)
        for e in range(8):
            moved = pltpu.roll(strips, (120 - 16 * e) % 128, 1)
            turn_ref[pl.ds(e, 32, stride=8), :] = all_ref[j, e] + jnp.where(ends, moved, 0.0)
        columns = pl.ds(128 * j, 128)
        total = turn_ref[...].reshape(32, 8, 128)
        out_ref[:, :, columns] = estimate_ref[:, :, columns] * (0.5 * total)


def finish(group, own, pieces, estimate, partial):
    slab = pl.BlockSpec((32, 8, 512), lambda g, s: (0, group(g), 0))
    more = [] if partial is None else [partial]
    return pl.pallas_call(
        finish_kernel,
        grid_spec=pltpu.PrefetchScalarGridSpec(
            num_scalar_prefetch=1,
            grid=(2,),
            in_specs=[PIECE_BLOCK] * 4 + [slab] + [pl.BlockSpec(memory_space=pl.ANY)] * len(more),
            out_specs=slab,
            scratch_shapes=[pltpu.VMEM((4, 9, 32, 128), F32), pltpu.VMEM((256, 128), F32)],
        ),
        out_shape=shape((32, 32, 512)),
        input_output_aliases={6: 0} if more else {},
        compiler_params=params(),
        cost_estimate=cost(2 << 20, 6 << 20),
        name="finish",
    )(own, *pieces, estimate, *more)


def send(value, pairs):
    return lax.ppermute(value, AXES, pairs)


def after(value, *others):
    return lax.optimization_barrier((value, *others))[0]


def on_device(estimate, observed, lateral_taps, axial_taps):
    lateral = lateral_taps / jnp.sum(lateral_taps, axis=2, keepdims=True)
    axial = axial_taps / jnp.sum(axial_taps, axis=1, keepdims=True)
    axial = jnp.pad(axial, ((0, 0), (0, 129)))
    wy = lateral[:, 1]
    gz, gy = lax.axis_index("gz"), lax.axis_index("gy")
    own = jnp.reshape(gz & 3, (1,))
    mask = jnp.reshape(32 * ((gz & 2) + (gy & 1)), (1,))

    packed = {k: pack(own ^ k, estimate) for k in ORDER}
    mine = {k: send(packed[k], to_block(k)) for k in ORDER}
    turned = {k: turn(after(own ^ k, *packed.values()), observed) for k in ORDER}
    near = {2: send(after(mine[2], *turned.values()), to_next_z(2)), 0: send(mine[0], to_next_z(0))}
    near[3] = send(after(mine[3], near[2]), to_next_z(3))
    near[1] = send(after(mine[1], near[0]), to_next_z(1))
    ready = {2: (mine[0],), 0: (mine[1], mine[3]), 3: (mine[1], near[3]), 1: (near[1], near[3])}
    seen = {k: send(after(turned[k], *ready[k]), to_block(k)) for k in ORDER}
    seen = [seen[k] for k in range(4)]
    z_taps, zt_taps, x_taps, xt_high, xt_low = weights(mask, lateral[:, 0], axial)

    pieces = [mine[k] for k in range(4)] + [near[k] for k in range(4)]
    blur_e, first, last = forward(edge_group, pieces, z_taps, x_taps, True)
    low, high = send(last, to_next_y(1)), send(first, to_next_y(-1))
    (blur_i,) = forward(inner_group, pieces, z_taps, x_taps, False)
    ratio_e, first, last = along_y(
        "ratio_e", EDGE_ROWS, False, wy, blur_e, blur_i, [low, high], seen
    )
    (ratio_i,) = along_y("ratio_i", INNER_ROWS, False, wy, blur_e, blur_i, [], seen)
    low, high = send(last, to_next_y(1)), send(first, to_next_y(-1))
    (back_i,) = along_y("back_i", INNER_ROWS, True, wy, ratio_e, ratio_i, [], [])
    parts_i = backward(back_i, xt_high, xt_low, zt_taps)
    (back_e,) = along_y("back_e", EDGE_ROWS, True, wy, ratio_e, ratio_i, [low, high], [])
    parts_e = backward(back_e, xt_high, xt_low, zt_taps)
    result = None
    for group, parts in ((inner_group, parts_i), (edge_group, parts_e)):
        outer = [send(parts[4 + pair], reverse(to_next_z(2 * pair))) for pair in range(2)]
        home = [
            send(parts[k] + outer[k // 2][k % 2], reverse(to_block(k))) for k in range(4)
        ]
        result = finish(group, own, home, estimate, result)
    return result


def solution(mesh):
    return jax.shard_map(
        on_device,
        mesh=mesh,
        in_specs=(P("gz", "gy", None), P(None, "gz", "gy", None), P(), P()),
        out_specs=P("gz", "gy", None),
        check_vma=False,
    )
```

```python
import jax
import jax.numpy as jnp
from jax import lax
from jax.experimental import pallas as pl
from jax.experimental.pallas import tpu as pltpu
from jax.sharding import PartitionSpec as P

AXES = ("gz", "gy")
F32 = jnp.float32
BF16 = jnp.bfloat16
VMEM_LIMIT = 24 * 1024 * 1024


def device(z, h, c, y, l):
    return ((z * 2 + h) * 2 + c) * 8 + y * 2 + l


def everyone():
    for z in range(4):
        for h in range(2):
            for c in range(2):
                for y in range(4):
                    for l in range(2):
                        yield z, h, c, y, l


def to_block(k):
    pairs = []
    for z, h, c, y, l in everyone():
        target = (2 * h + c) ^ k
        pairs.append((device(z, h, c, y, l), device(z, target >> 1, l, y, target & 1)))
    return pairs


def to_next_z(k):
    pairs = []
    for z, h, c, y, l in everyone():
        other = z - 1 if (h ^ (k >> 1)) == 0 else z + 1
        if 0 <= other < 4:
            pairs.append((device(z, h, c, y, l), device(other, h, c, y, l)))
    return pairs


def to_next_y(step):
    pairs = []
    for z, h, c, y, l in everyone():
        run = 2 * y + c + step
        if 0 <= run < 8:
            pairs.append((device(z, h, c, y, l), device(z, h, run & 1, run >> 1, l)))
    return pairs


def reverse(pairs):
    return [(target, source) for source, target in pairs]


def halves(value):
    high = value.astype(BF16)
    low = (value - high.astype(F32)).astype(BF16)
    return high, low


def mxu(left, right):
    return jnp.dot(left, right, preferred_element_type=F32)


def shape(dims, dtype=F32):
    return jax.ShapeDtypeStruct(dims, dtype)


def whole(dims):
    return pl.BlockSpec(dims, lambda *_: (0,) * len(dims))


SMEM = pl.BlockSpec(memory_space=pltpu.SMEM)
PIECE = (2, 9, 32, 128)
WHOLE_PIECE = (4, 9, 32, 128)
PIECE_BLOCK = pl.BlockSpec((1, 9, 32, 128), lambda g, *_: (g, 0, 0, 0))


def edge_group(g):
    return 3 * g


def inner_group(g):
    return g + 1


ORDER = (2, 0, 3, 1)
EDGE_ROWS = list(range(0, 8)) + list(range(24, 32))
INNER_ROWS = list(range(8, 24))


def params():
    return pltpu.CompilerParams(vmem_limit_bytes=VMEM_LIMIT)


def cost(flops, count):
    return pl.CostEstimate(flops=1024, bytes_accessed=1024, transcendentals=0)


def pack_kernel(column_ref, centre_ref, left_ref, right_ref, out_ref):
    column = column_ref[0]
    lane = lax.broadcasted_iota(jnp.int32, (32, 128), 1)
    take_left = jnp.logical_and(lane >= 120, column > 0)
    take_right = jnp.logical_and(lane < 8, column < 3)
    centre = centre_ref.reshape(256, 128)
    left = left_ref.reshape(256, 128)
    right = right_ref.reshape(256, 128)
    strips = jnp.zeros((32, 128), F32)
    for e in range(8):
        rows = pl.ds(e, 32, stride=8)
        out_ref[0, e] = centre[rows, :]
        edge = jnp.where(take_left, left[rows, :], jnp.where(take_right, right[rows, :], 0.0))
        strips = strips + pltpu.roll(edge, (16 * e + 8) % 128, 1)
    out_ref[0, 8] = strips


def pack(column, estimate):
    block = (32, 8, 128)
    return pl.pallas_call(
        pack_kernel,
        grid_spec=pltpu.PrefetchScalarGridSpec(
            num_scalar_prefetch=1,
            grid=(4,),
            in_specs=[
                pl.BlockSpec(block, lambda g, s: (0, g, s[0])),
                pl.BlockSpec(block, lambda g, s: (0, g, jnp.maximum(s[0] - 1, 0))),
                pl.BlockSpec(block, lambda g, s: (0, g, jnp.minimum(s[0] + 1, 3))),
            ],
            out_specs=PIECE_BLOCK,
        ),
        out_shape=shape(WHOLE_PIECE),
        compiler_params=params(),
        cost_estimate=cost(1 << 20, 12 << 20),
        name="pack",
    )(column, estimate, estimate, estimate)


def turn_kernel(column_ref, in_ref, out_ref):
    for v in range(2):
        rows = in_ref.at[v].reshape(256, 128)
        for e in range(8):
            out_ref[v, e] = rows[pl.ds(e, 32, stride=8), :]


def turn(column, observed):
    return pl.pallas_call(
        turn_kernel,
        grid_spec=pltpu.PrefetchScalarGridSpec(
            num_scalar_prefetch=1,
            grid=(4,),
            in_specs=[pl.BlockSpec((2, 32, 8, 128), lambda g, s: (0, 0, g, s[0]))],
            out_specs=pl.BlockSpec((2, 8, 32, 128), lambda g, s: (0, g, 0, 0)),
        ),
        out_shape=shape((2, 32, 32, 128)),
        compiler_params=params(),
        cost_estimate=cost(1 << 20, 6 << 20),
        name="turn",
    )(column, observed)


def weights_kernel(mask_ref, wx_ref, wz_ref, z_ref, zt_ref, x_ref, xth_ref, xtl_ref):
    mask = mask_ref[0]
    row = lax.broadcasted_iota(jnp.int32, (128, 256), 0) ^ mask
    lane = lax.broadcasted_iota(jnp.int32, (128, 256), 1)
    parts = []
    for v in range(2):
        band = jnp.broadcast_to(wz_ref[v : v + 1, :], (128, 256))
        band = pltpu.roll(band, 256 - 63, 1)
        for bit in range(7):
            step = 1 << bit
            band = jnp.where((row & step) != 0, pltpu.roll(band, step, 1), band)
        for step in (32, 64):
            other = jnp.where(
                (lane & step) == 0, pltpu.roll(band, 256 - step, 1), pltpu.roll(band, step, 1)
            )
            band = jnp.where(((lane * 0 + mask) & step) != 0, other, band)
        parts.append(band)
    full = jnp.concatenate(parts, axis=0)
    high, low = halves(full)
    z_ref[:, 0:256] = high
    z_ref[:, 256:512] = low
    z_ref[:, 512:768] = high
    high, low = halves(full.T)
    zt_ref[:, 0:256] = high
    zt_ref[:, 256:512] = low
    zt_ref[:, 512:768] = high

    def x_taps(dims, column_dim, v):
        spot = lax.broadcasted_iota(jnp.int32, dims, column_dim)
        own = lax.broadcasted_iota(jnp.int32, dims, 1 - column_dim)
        strip = spot & 15
        column = jnp.where(spot < 128, spot + 8, jnp.where(strip < 8, strip, strip + 128))
        tap = column - own - 1
        total = jnp.zeros(dims, F32)
        for t in range(15):
            total = jnp.where(tap == t, wx_ref[v, t], total)
        return spot, total

    for v in range(2):
        spot, total = x_taps((256, 128), 0, v)
        for e in range(8):
            keep = jnp.logical_or(spot < 128, (spot - 128) // 16 == e)
            high, low = halves(jnp.where(keep, total, 0.0))
            x_ref[v, e, :, 0:128] = high
            x_ref[v, e, :, 128:256] = low
        spot, total = x_taps((128, 256), 1, v)
        for e in range(8):
            keep = jnp.logical_or(spot < 128, (spot - 128) // 16 == e)
            high, low = halves(jnp.where(keep, total, 0.0))
            xth_ref[v, e] = high
            xtl_ref[v, e] = low


def weights(mask, wx, wz):
    outs = [
        shape((256, 768), BF16),
        shape((256, 768), BF16),
        shape((2, 8, 256, 256), BF16),
        shape((2, 8, 128, 256), BF16),
        shape((2, 8, 128, 256), BF16),
    ]
    return pl.pallas_call(
        weights_kernel,
        in_specs=[SMEM, SMEM, pl.BlockSpec(memory_space=pltpu.VMEM)],
        out_specs=[pl.BlockSpec(memory_space=pltpu.VMEM)] * 5,
        out_shape=outs,
        compiler_params=params(),
        cost_estimate=cost(1 << 24, 16 << 20),
        name="weights",
    )(mask, wx, wz)


def forward_kernel(*refs):
    pieces = refs[:8]
    z_ref, x_ref, out_ref = refs[8:11]
    z_taps = z_ref[...]

    def along_z(rows):
        lines = [jnp.concatenate([ref[0, row] for ref in pieces], axis=0) for row in rows]
        field = jnp.concatenate(lines, axis=1) if len(lines) > 1 else lines[0]
        high, low = halves(field)
        return mxu(z_taps, jnp.concatenate([high, high, low], axis=0))

    strips = along_z([8])
    strip_halves = [halves(strips[128 * v : 128 * v + 128]) for v in range(2)]
    for pair in range(4):
        both = along_z([2 * pair, 2 * pair + 1])
        for at in range(2):
            e = 2 * pair + at
            for v in range(2):
                high, low = halves(both[128 * v : 128 * v + 128, 128 * at : 128 * at + 128])
                high = jnp.concatenate([high, strip_halves[v][0]], axis=1)
                low = jnp.concatenate([low, strip_halves[v][1]], axis=1)
                first = mxu(high, x_ref[v, e])
                second = mxu(low, x_ref[v, e, :, 0:128])
                out_ref[v, e] = (first[:, 0:128] + first[:, 128:256]) + second
    if len(refs) > 11:
        first_ref, last_ref = refs[11:]

        @pl.when(pl.program_id(0) == 0)
        def _():
            first_ref[...] = out_ref[:, 0:7]

        @pl.when(pl.program_id(0) == 1)
        def _():
            last_ref[...] = out_ref[:, 1:8]


def forward(group, pieces, z_taps, x_taps, edges):
    out_specs = [pl.BlockSpec((2, 8, 128, 128), lambda g: (0, g, 0, 0))]
    out_shape = [shape((2, 16, 128, 128))]
    if edges:
        out_specs += [whole((2, 7, 128, 128))] * 2
        out_shape += [shape((2, 7, 128, 128))] * 2
    return pl.pallas_call(
        forward_kernel,
        grid=(2,),
        in_specs=[pl.BlockSpec((1, 9, 32, 128), lambda g: (group(g), 0, 0, 0))] * 8
        + [whole((256, 768)), whole((2, 8, 256, 256))],
        out_specs=out_specs,
        out_shape=out_shape,
        compiler_params=params(),
        cost_estimate=cost(4 << 30, 12 << 20),
        name="forward",
    )(*pieces, z_taps, x_taps)


def y_kernel(rows, flip, with_edges, with_ratio):
    def kernel(wy_ref, edge_ref, inner_ref, *refs):
        refs = list(refs)
        low_ref, high_ref = (refs.pop(0), refs.pop(0)) if with_edges else (None, None)
        observed = [refs.pop(0) for _ in range(4)] if with_ratio else []
        out_ref = refs.pop(0)
        v = pl.program_id(0)
        taps = [wy_ref[v, 14 - t if flip else t] for t in range(15)]

        def sums(start, store):
            def line(row):
                part = pl.ds(start, 8)
                if row < 0:
                    return low_ref[0, row + 7, part, :]
                if row < 8:
                    return edge_ref[0, row, part, :]
                if row < 24:
                    return inner_ref[0, row - 8, part, :]
                if row < 32:
                    return edge_ref[0, row - 16, part, :]
                return high_ref[0, row - 32, part, :]

            for at, row in enumerate(rows):
                total = taps[0] * line(row - 7)
                for t in range(1, 15):
                    total = total + taps[t] * line(row + t - 7)
                store(at, row, total)

        if not with_ratio:

            @pl.loop(0, 16)
            def _(part):
                start = pl.multiple_of(part * 8, 8)

                def store(at, row, total):
                    out_ref[0, at, pl.ds(start, 8), :] = total

                sums(start, store)

            return

        for k in range(4):

            @pl.loop(0, 4)
            def _(part, k=k):
                inner = pl.multiple_of(part * 8, 8)
                start = pl.multiple_of(32 * k + part * 8, 8)

                def store(at, row, total):
                    ratio = observed[k][0, row, pl.ds(inner, 8), :] / total
                    out_ref[0, at, pl.ds(start, 8), :] = ratio
                    if with_edges and row < 7:
                        refs[0][0, row, pl.ds(start, 8), :] = ratio
                    if with_edges and row > 24:
                        refs[1][0, row - 25, pl.ds(start, 8), :] = ratio

                sums(start, store)

    return kernel


def along_y(name, rows, flip, wy, edge, inner, outer, observed):
    seven = pl.BlockSpec((1, 7, 128, 128), lambda v: (v, 0, 0, 0))
    chunk = pl.BlockSpec((1, 16, 128, 128), lambda v: (v, 0, 0, 0))
    quarter = pl.BlockSpec((1, 32, 32, 128), lambda v: (v, 0, 0, 0))
    gives_edges = len(outer) > 0 and len(observed) > 0
    return pl.pallas_call(
        y_kernel(rows, flip, len(outer) > 0, len(observed) > 0),
        grid=(2,),
        in_specs=[SMEM, chunk, chunk] + [seven] * len(outer) + [quarter] * len(observed),
        out_specs=[chunk] + [seven] * (2 * gives_edges),
        out_shape=[shape((2, 16, 128, 128))] + [shape((2, 7, 128, 128))] * (2 * gives_edges),
        compiler_params=params(),
        cost_estimate=cost(15 << 20, 12 << 20),
        name=name,
    )(wy, edge, inner, *outer, *observed)


def backward_kernel(in_ref, xth_ref, xtl_ref, zt_ref, *outs):
    zt_taps = zt_ref[...]

    def along_z(fields, rows):
        high, low = halves(jnp.concatenate(fields, axis=1) if len(fields) > 1 else fields[0])
        result = mxu(zt_taps, jnp.concatenate([high, high, low], axis=0))
        for at, row in enumerate(rows):
            for m in range(8):
                part = result[32 * m : 32 * m + 32, 128 * at : 128 * at + 128]
                if m < 4:
                    outs[m][0, row] = part
                else:
                    outs[4 + (m - 4) // 2][m % 2, 0, row] = part

    strips = [jnp.zeros((128, 128), F32), jnp.zeros((128, 128), F32)]
    for pair in range(4):
        fields = []
        for e in (2 * pair, 2 * pair + 1):
            mains = []
            for v in range(2):
                high, low = halves(in_ref[v, e])
                right = xth_ref[v, e]
                wide = mxu(
                    jnp.concatenate([high, low], axis=1), jnp.concatenate([right, right], axis=0)
                ) + mxu(high, xtl_ref[v, e])
                mains.append(wide[:, 0:128])
                strips[v] = strips[v] + wide[:, 128:256]
            fields.append(jnp.concatenate(mains, axis=0))
        along_z(fields, [2 * pair, 2 * pair + 1])
    along_z([jnp.concatenate(strips, axis=0)], [8])


def backward(field, xt_high, xt_low, zt_taps):
    return pl.pallas_call(
        backward_kernel,
        grid=(2,),
        in_specs=[
            pl.BlockSpec((2, 8, 128, 128), lambda g: (0, g, 0, 0)),
            whole((2, 8, 128, 256)),
            whole((2, 8, 128, 256)),
            whole((256, 768)),
        ],
        out_specs=[PIECE_BLOCK] * 4
        + [pl.BlockSpec((2, 1, 9, 32, 128), lambda g: (0, g, 0, 0, 0))] * 2,
        out_shape=[shape(PIECE)] * 4 + [shape((2,) + PIECE)] * 2,
        compiler_params=params(),
        cost_estimate=cost(4 << 30, 12 << 20),
        name="backward",
    )(field, xt_high, xt_low, zt_taps)


def finish_kernel(own_ref, p0, p1, p2, p3, estimate_ref, *refs):
    out_ref, all_ref, turn_ref = refs[-3:]
    own = own_ref[0]
    for k, ref in enumerate((p0, p1, p2, p3)):
        all_ref[own ^ k] = ref[0]
    lane = lax.broadcasted_iota(jnp.int32, (32, 128), 1)
    ends = jnp.logical_or(lane >= 120, lane < 8)
    from_next = (lane & 8) == 0
    for j in range(4):
        zero = jnp.zeros((32, 128), F32)
        after = all_ref[j + 1, 8] if j < 3 else zero
        before = all_ref[j - 1, 8] if j > 0 else zero
        strips = jnp.where(from_next, after, before)
        for e in range(8):
            moved = pltpu.roll(strips, (120 - 16 * e) % 128, 1)
            turn_ref[pl.ds(e, 32, stride=8), :] = all_ref[j, e] + jnp.where(ends, moved, 0.0)
        columns = pl.ds(128 * j, 128)
        total = turn_ref[...].reshape(32, 8, 128)
        out_ref[:, :, columns] = estimate_ref[:, :, columns] * (0.5 * total)


def finish(group, own, pieces, estimate, partial):
    slab = pl.BlockSpec((32, 8, 512), lambda g, s: (0, group(g), 0))
    more = [] if partial is None else [partial]
    return pl.pallas_call(
        finish_kernel,
        grid_spec=pltpu.PrefetchScalarGridSpec(
            num_scalar_prefetch=1,
            grid=(2,),
            in_specs=[PIECE_BLOCK] * 4 + [slab] + [pl.BlockSpec(memory_space=pl.ANY)] * len(more),
            out_specs=slab,
            scratch_shapes=[pltpu.VMEM((4, 9, 32, 128), F32), pltpu.VMEM((256, 128), F32)],
        ),
        out_shape=shape((32, 32, 512)),
        input_output_aliases={6: 0} if more else {},
        compiler_params=params(),
        cost_estimate=cost(2 << 20, 6 << 20),
        name="finish",
    )(own, *pieces, estimate, *more)


def send(value, pairs):
    return lax.ppermute(value, AXES, pairs)


def after(value, *others):
    return lax.optimization_barrier((value, *others))[0]


def on_device(estimate, observed, lateral_taps, axial_taps):
    lateral = lateral_taps / jnp.sum(lateral_taps, axis=2, keepdims=True)
    axial = axial_taps / jnp.sum(axial_taps, axis=1, keepdims=True)
    axial = jnp.pad(axial, ((0, 0), (0, 129)))
    wy = lateral[:, 1]
    gz, gy = lax.axis_index("gz"), lax.axis_index("gy")
    own = jnp.reshape(gz & 3, (1,))
    mask = jnp.reshape(32 * ((gz & 2) + (gy & 1)), (1,))

    packed = {}
    for k in ORDER:
        packed[k] = pack(after(own ^ k, *packed.values()), estimate)
    mine = {k: send(packed[k], to_block(k)) for k in ORDER}
    turned = {k: turn(after(own ^ k, *packed.values()), observed) for k in ORDER}
    seen = {2: send(turned[2], to_block(2)), 3: send(turned[3], to_block(3))}
    seen[0] = send(turned[0], to_block(0))
    seen[1] = send(turned[1], to_block(1))
    near = {2: send(after(mine[2], *turned.values()), to_next_z(2)), 0: send(after(mine[0], *turned.values()), to_next_z(0))}
    near[3] = send(after(mine[3], near[2]), to_next_z(3))
    near[1] = send(after(mine[1], near[0]), to_next_z(1))
    seen = [seen[k] for k in range(4)]
    z_taps, zt_taps, x_taps, xt_high, xt_low = weights(mask, lateral[:, 0], axial)

    pieces = [mine[k] for k in range(4)] + [near[k] for k in range(4)]
    blur_e, first, last = forward(edge_group, pieces, z_taps, x_taps, True)
    low, high = send(last, to_next_y(1)), send(first, to_next_y(-1))
    (blur_i,) = forward(inner_group, pieces, z_taps, x_taps, False)
    ratio_e, first, last = along_y(
        "ratio_e", EDGE_ROWS, False, wy, blur_e, blur_i, [low, high], seen
    )
    (ratio_i,) = along_y("ratio_i", INNER_ROWS, False, wy, blur_e, blur_i, [], seen)
    low, high = send(last, to_next_y(1)), send(first, to_next_y(-1))
    (back_i,) = along_y("back_i", INNER_ROWS, True, wy, ratio_e, ratio_i, [], [])
    parts_i = backward(back_i, xt_high, xt_low, zt_taps)
    (back_e,) = along_y("back_e", EDGE_ROWS, True, wy, ratio_e, ratio_i, [low, high], [])
    parts_e = backward(back_e, xt_high, xt_low, zt_taps)
    result = None
    for group, parts in ((inner_group, parts_i), (edge_group, parts_e)):
        outer = [send(parts[4 + pair], reverse(to_next_z(2 * pair))) for pair in range(2)]
        home = [
            send(parts[k] + outer[k // 2][k % 2], reverse(to_block(k))) for k in range(4)
        ]
        result = finish(group, own, home, estimate, result)
    return result


def solution(mesh):
    return jax.shard_map(
        on_device,
        mesh=mesh,
        in_specs=(P("gz", "gy", None), P(None, "gz", "gy", None), P(), P()),
        out_specs=P("gz", "gy", None),
        check_vma=False,
    )
```

```python
import jax
import jax.numpy as jnp
from jax import lax
from jax.experimental import pallas as pl
from jax.experimental.pallas import tpu as pltpu
from jax.sharding import PartitionSpec as P

AXES = ("gz", "gy")
F32 = jnp.float32
BF16 = jnp.bfloat16
VMEM_LIMIT = 24 * 1024 * 1024


def device(z, h, c, y, l):
    return ((z * 2 + h) * 2 + c) * 8 + y * 2 + l


def everyone():
    for z in range(4):
        for h in range(2):
            for c in range(2):
                for y in range(4):
                    for l in range(2):
                        yield z, h, c, y, l


def to_block(k):
    pairs = []
    for z, h, c, y, l in everyone():
        target = (2 * h + c) ^ k
        pairs.append((device(z, h, c, y, l), device(z, target >> 1, l, y, target & 1)))
    return pairs


def to_next_z(k):
    pairs = []
    for z, h, c, y, l in everyone():
        other = z - 1 if (h ^ (k >> 1)) == 0 else z + 1
        if 0 <= other < 4:
            pairs.append((device(z, h, c, y, l), device(other, h, c, y, l)))
    return pairs


def to_next_y(step):
    pairs = []
    for z, h, c, y, l in everyone():
        run = 2 * y + c + step
        if 0 <= run < 8:
            pairs.append((device(z, h, c, y, l), device(z, h, run & 1, run >> 1, l)))
    return pairs


def reverse(pairs):
    return [(target, source) for source, target in pairs]


def halves(value):
    high = value.astype(BF16)
    low = (value - high.astype(F32)).astype(BF16)
    return high, low


def mxu(left, right):
    return jnp.dot(left, right, preferred_element_type=F32)


def shape(dims, dtype=F32):
    return jax.ShapeDtypeStruct(dims, dtype)


def whole(dims):
    return pl.BlockSpec(dims, lambda *_: (0,) * len(dims))


SMEM = pl.BlockSpec(memory_space=pltpu.SMEM)
PIECE = (2, 9, 32, 128)
WHOLE_PIECE = (4, 9, 32, 128)
PIECE_BLOCK = pl.BlockSpec((1, 9, 32, 128), lambda g, *_: (g, 0, 0, 0))


def edge_group(g):
    return 3 * g


def inner_group(g):
    return g + 1


ORDER = (0, 2, 1, 3)
EDGE_ROWS = list(range(0, 8)) + list(range(24, 32))
INNER_ROWS = list(range(8, 24))


def params():
    return pltpu.CompilerParams(vmem_limit_bytes=VMEM_LIMIT)


def cost(flops, count):
    return pl.CostEstimate(flops=1024, bytes_accessed=1024, transcendentals=0)


def pack_kernel(column_ref, centre_ref, left_ref, right_ref, out_ref):
    column = column_ref[0]
    lane = lax.broadcasted_iota(jnp.int32, (32, 128), 1)
    take_left = jnp.logical_and(lane >= 120, column > 0)
    take_right = jnp.logical_and(lane < 8, column < 3)
    centre = centre_ref.reshape(256, 128)
    left = left_ref.reshape(256, 128)
    right = right_ref.reshape(256, 128)
    strips = jnp.zeros((32, 128), F32)
    for e in range(8):
        rows = pl.ds(e, 32, stride=8)
        out_ref[0, e] = centre[rows, :]
        edge = jnp.where(take_left, left[rows, :], jnp.where(take_right, right[rows, :], 0.0))
        strips = strips + pltpu.roll(edge, (16 * e + 8) % 128, 1)
    out_ref[0, 8] = strips


def pack(column, estimate):
    block = (32, 8, 128)
    return pl.pallas_call(
        pack_kernel,
        grid_spec=pltpu.PrefetchScalarGridSpec(
            num_scalar_prefetch=1,
            grid=(4,),
            in_specs=[
                pl.BlockSpec(block, lambda g, s: (0, g, s[0])),
                pl.BlockSpec(block, lambda g, s: (0, g, jnp.maximum(s[0] - 1, 0))),
                pl.BlockSpec(block, lambda g, s: (0, g, jnp.minimum(s[0] + 1, 3))),
            ],
            out_specs=PIECE_BLOCK,
        ),
        out_shape=shape(WHOLE_PIECE),
        compiler_params=params(),
        cost_estimate=cost(1 << 20, 12 << 20),
        name="pack",
    )(column, estimate, estimate, estimate)


def turn_kernel(column_ref, in_ref, out_ref):
    for v in range(2):
        rows = in_ref.at[v].reshape(256, 128)
        for e in range(8):
            out_ref[v, e] = rows[pl.ds(e, 32, stride=8), :]


def turn(column, observed):
    return pl.pallas_call(
        turn_kernel,
        grid_spec=pltpu.PrefetchScalarGridSpec(
            num_scalar_prefetch=1,
            grid=(4,),
            in_specs=[pl.BlockSpec((2, 32, 8, 128), lambda g, s: (0, 0, g, s[0]))],
            out_specs=pl.BlockSpec((2, 8, 32, 128), lambda g, s: (0, g, 0, 0)),
        ),
        out_shape=shape((2, 32, 32, 128)),
        compiler_params=params(),
        cost_estimate=cost(1 << 20, 6 << 20),
        name="turn",
    )(column, observed)


def weights_kernel(mask_ref, wx_ref, wz_ref, z_ref, zt_ref, x_ref, xth_ref, xtl_ref):
    mask = mask_ref[0]
    row = lax.broadcasted_iota(jnp.int32, (128, 256), 0) ^ mask
    lane = lax.broadcasted_iota(jnp.int32, (128, 256), 1)
    parts = []
    for v in range(2):
        band = jnp.broadcast_to(wz_ref[v : v + 1, :], (128, 256))
        band = pltpu.roll(band, 256 - 63, 1)
        for bit in range(7):
            step = 1 << bit
            band = jnp.where((row & step) != 0, pltpu.roll(band, step, 1), band)
        for step in (32, 64):
            other = jnp.where(
                (lane & step) == 0, pltpu.roll(band, 256 - step, 1), pltpu.roll(band, step, 1)
            )
            band = jnp.where(((lane * 0 + mask) & step) != 0, other, band)
        parts.append(band)
    full = jnp.concatenate(parts, axis=0)
    high, low = halves(full)
    z_ref[:, 0:256] = high
    z_ref[:, 256:512] = low
    z_ref[:, 512:768] = high
    high, low = halves(full.T)
    zt_ref[:, 0:256] = high
    zt_ref[:, 256:512] = low
    zt_ref[:, 512:768] = high

    def x_taps(dims, column_dim, v):
        spot = lax.broadcasted_iota(jnp.int32, dims, column_dim)
        own = lax.broadcasted_iota(jnp.int32, dims, 1 - column_dim)
        strip = spot & 15
        column = jnp.where(spot < 128, spot + 8, jnp.where(strip < 8, strip, strip + 128))
        tap = column - own - 1
        total = jnp.zeros(dims, F32)
        for t in range(15):
            total = jnp.where(tap == t, wx_ref[v, t], total)
        return spot, total

    for v in range(2):
        spot, total = x_taps((256, 128), 0, v)
        for e in range(8):
            keep = jnp.logical_or(spot < 128, (spot - 128) // 16 == e)
            high, low = halves(jnp.where(keep, total, 0.0))
            x_ref[v, e, :, 0:128] = high
            x_ref[v, e, :, 128:256] = low
        spot, total = x_taps((128, 256), 1, v)
        for e in range(8):
            keep = jnp.logical_or(spot < 128, (spot - 128) // 16 == e)
            high, low = halves(jnp.where(keep, total, 0.0))
            xth_ref[v, e] = high
            xtl_ref[v, e] = low


def weights(mask, wx, wz):
    outs = [
        shape((256, 768), BF16),
        shape((256, 768), BF16),
        shape((2, 8, 256, 256), BF16),
        shape((2, 8, 128, 256), BF16),
        shape((2, 8, 128, 256), BF16),
    ]
    return pl.pallas_call(
        weights_kernel,
        in_specs=[SMEM, SMEM, pl.BlockSpec(memory_space=pltpu.VMEM)],
        out_specs=[pl.BlockSpec(memory_space=pltpu.VMEM)] * 5,
        out_shape=outs,
        compiler_params=params(),
        cost_estimate=cost(1 << 24, 16 << 20),
        name="weights",
    )(mask, wx, wz)


def forward_kernel(*refs):
    pieces = refs[:8]
    z_ref, x_ref, out_ref = refs[8:11]
    z_taps = z_ref[...]

    def along_z(rows):
        lines = [jnp.concatenate([ref[0, row] for ref in pieces], axis=0) for row in rows]
        field = jnp.concatenate(lines, axis=1) if len(lines) > 1 else lines[0]
        high, low = halves(field)
        return mxu(z_taps, jnp.concatenate([high, high, low], axis=0))

    strips = along_z([8])
    strip_halves = [halves(strips[128 * v : 128 * v + 128]) for v in range(2)]
    for pair in range(4):
        both = along_z([2 * pair, 2 * pair + 1])
        for at in range(2):
            e = 2 * pair + at
            for v in range(2):
                high, low = halves(both[128 * v : 128 * v + 128, 128 * at : 128 * at + 128])
                high = jnp.concatenate([high, strip_halves[v][0]], axis=1)
                low = jnp.concatenate([low, strip_halves[v][1]], axis=1)
                first = mxu(high, x_ref[v, e])
                second = mxu(low, x_ref[v, e, :, 0:128])
                out_ref[v, e] = (first[:, 0:128] + first[:, 128:256]) + second
    if len(refs) > 11:
        first_ref, last_ref = refs[11:]

        @pl.when(pl.program_id(0) == 0)
        def _():
            first_ref[...] = out_ref[:, 0:7]

        @pl.when(pl.program_id(0) == 1)
        def _():
            last_ref[...] = out_ref[:, 1:8]


def forward(group, pieces, z_taps, x_taps, edges):
    out_specs = [pl.BlockSpec((2, 8, 128, 128), lambda g: (0, g, 0, 0))]
    out_shape = [shape((2, 16, 128, 128))]
    if edges:
        out_specs += [whole((2, 7, 128, 128))] * 2
        out_shape += [shape((2, 7, 128, 128))] * 2
    return pl.pallas_call(
        forward_kernel,
        grid=(2,),
        in_specs=[pl.BlockSpec((1, 9, 32, 128), lambda g: (group(g), 0, 0, 0))] * 8
        + [whole((256, 768)), whole((2, 8, 256, 256))],
        out_specs=out_specs,
        out_shape=out_shape,
        compiler_params=params(),
        cost_estimate=cost(4 << 30, 12 << 20),
        name="forward",
    )(*pieces, z_taps, x_taps)


def y_kernel(rows, flip, with_edges, with_ratio):
    def kernel(wy_ref, edge_ref, inner_ref, *refs):
        refs = list(refs)
        low_ref, high_ref = (refs.pop(0), refs.pop(0)) if with_edges else (None, None)
        observed = [refs.pop(0) for _ in range(4)] if with_ratio else []
        out_ref = refs.pop(0)
        v = pl.program_id(0)
        taps = [wy_ref[v, 14 - t if flip else t] for t in range(15)]

        def sums(start, store):
            def line(row):
                part = pl.ds(start, 8)
                if row < 0:
                    return low_ref[0, row + 7, part, :]
                if row < 8:
                    return edge_ref[0, row, part, :]
                if row < 24:
                    return inner_ref[0, row - 8, part, :]
                if row < 32:
                    return edge_ref[0, row - 16, part, :]
                return high_ref[0, row - 32, part, :]

            for at, row in enumerate(rows):
                total = taps[0] * line(row - 7)
                for t in range(1, 15):
                    total = total + taps[t] * line(row + t - 7)
                store(at, row, total)

        if not with_ratio:

            @pl.loop(0, 16)
            def _(part):
                start = pl.multiple_of(part * 8, 8)

                def store(at, row, total):
                    out_ref[0, at, pl.ds(start, 8), :] = total

                sums(start, store)

            return

        for k in range(4):

            @pl.loop(0, 4)
            def _(part, k=k):
                inner = pl.multiple_of(part * 8, 8)
                start = pl.multiple_of(32 * k + part * 8, 8)

                def store(at, row, total):
                    ratio = observed[k][0, row, pl.ds(inner, 8), :] / total
                    out_ref[0, at, pl.ds(start, 8), :] = ratio
                    if with_edges and row < 7:
                        refs[0][0, row, pl.ds(start, 8), :] = ratio
                    if with_edges and row > 24:
                        refs[1][0, row - 25, pl.ds(start, 8), :] = ratio

                sums(start, store)

    return kernel


def along_y(name, rows, flip, wy, edge, inner, outer, observed):
    seven = pl.BlockSpec((1, 7, 128, 128), lambda v: (v, 0, 0, 0))
    chunk = pl.BlockSpec((1, 16, 128, 128), lambda v: (v, 0, 0, 0))
    quarter = pl.BlockSpec((1, 32, 32, 128), lambda v: (v, 0, 0, 0))
    gives_edges = len(outer) > 0 and len(observed) > 0
    return pl.pallas_call(
        y_kernel(rows, flip, len(outer) > 0, len(observed) > 0),
        grid=(2,),
        in_specs=[SMEM, chunk, chunk] + [seven] * len(outer) + [quarter] * len(observed),
        out_specs=[chunk] + [seven] * (2 * gives_edges),
        out_shape=[shape((2, 16, 128, 128))] + [shape((2, 7, 128, 128))] * (2 * gives_edges),
        compiler_params=params(),
        cost_estimate=cost(15 << 20, 12 << 20),
        name=name,
    )(wy, edge, inner, *outer, *observed)


def backward_kernel(in_ref, xth_ref, xtl_ref, zt_ref, *outs):
    zt_taps = zt_ref[...]

    def along_z(fields, rows):
        high, low = halves(jnp.concatenate(fields, axis=1) if len(fields) > 1 else fields[0])
        result = mxu(zt_taps, jnp.concatenate([high, high, low], axis=0))
        for at, row in enumerate(rows):
            for m in range(8):
                part = result[32 * m : 32 * m + 32, 128 * at : 128 * at + 128]
                if m < 4:
                    outs[m][0, row] = part
                else:
                    outs[4 + (m - 4) // 2][m % 2, 0, row] = part

    strips = [jnp.zeros((128, 128), F32), jnp.zeros((128, 128), F32)]
    for pair in range(4):
        fields = []
        for e in (2 * pair, 2 * pair + 1):
            mains = []
            for v in range(2):
                high, low = halves(in_ref[v, e])
                right = xth_ref[v, e]
                wide = mxu(
                    jnp.concatenate([high, low], axis=1), jnp.concatenate([right, right], axis=0)
                ) + mxu(high, xtl_ref[v, e])
                mains.append(wide[:, 0:128])
                strips[v] = strips[v] + wide[:, 128:256]
            fields.append(jnp.concatenate(mains, axis=0))
        along_z(fields, [2 * pair, 2 * pair + 1])
    along_z([jnp.concatenate(strips, axis=0)], [8])


def backward(field, xt_high, xt_low, zt_taps):
    return pl.pallas_call(
        backward_kernel,
        grid=(2,),
        in_specs=[
            pl.BlockSpec((2, 8, 128, 128), lambda g: (0, g, 0, 0)),
            whole((2, 8, 128, 256)),
            whole((2, 8, 128, 256)),
            whole((256, 768)),
        ],
        out_specs=[PIECE_BLOCK] * 4
        + [pl.BlockSpec((2, 1, 9, 32, 128), lambda g: (0, g, 0, 0, 0))] * 2,
        out_shape=[shape(PIECE)] * 4 + [shape((2,) + PIECE)] * 2,
        compiler_params=params(),
        cost_estimate=cost(4 << 30, 12 << 20),
        name="backward",
    )(field, xt_high, xt_low, zt_taps)


def finish_kernel(own_ref, p0, p1, p2, p3, estimate_ref, *refs):
    out_ref, all_ref, turn_ref = refs[-3:]
    own = own_ref[0]
    for k, ref in enumerate((p0, p1, p2, p3)):
        all_ref[own ^ k] = ref[0]
    lane = lax.broadcasted_iota(jnp.int32, (32, 128), 1)
    ends = jnp.logical_or(lane >= 120, lane < 8)
    from_next = (lane & 8) == 0
    for j in range(4):
        zero = jnp.zeros((32, 128), F32)
        after = all_ref[j + 1, 8] if j < 3 else zero
        before = all_ref[j - 1, 8] if j > 0 else zero
        strips = jnp.where(from_next, after, before)
        for e in range(8):
            moved = pltpu.roll(strips, (120 - 16 * e) % 128, 1)
            turn_ref[pl.ds(e, 32, stride=8), :] = all_ref[j, e] + jnp.where(ends, moved, 0.0)
        columns = pl.ds(128 * j, 128)
        total = turn_ref[...].reshape(32, 8, 128)
        out_ref[:, :, columns] = estimate_ref[:, :, columns] * (0.5 * total)


def finish(group, own, pieces, estimate, partial):
    slab = pl.BlockSpec((32, 8, 512), lambda g, s: (0, group(g), 0))
    more = [] if partial is None else [partial]
    return pl.pallas_call(
        finish_kernel,
        grid_spec=pltpu.PrefetchScalarGridSpec(
            num_scalar_prefetch=1,
            grid=(2,),
            in_specs=[PIECE_BLOCK] * 4 + [slab] + [pl.BlockSpec(memory_space=pl.ANY)] * len(more),
            out_specs=slab,
            scratch_shapes=[pltpu.VMEM((4, 9, 32, 128), F32), pltpu.VMEM((256, 128), F32)],
        ),
        out_shape=shape((32, 32, 512)),
        input_output_aliases={6: 0} if more else {},
        compiler_params=params(),
        cost_estimate=cost(2 << 20, 6 << 20),
        name="finish",
    )(own, *pieces, estimate, *more)


def send(value, pairs):
    return lax.ppermute(value, AXES, pairs)


def after(value, *others):
    return lax.optimization_barrier((value, *others))[0]


def on_device(estimate, observed, lateral_taps, axial_taps):
    lateral = lateral_taps / jnp.sum(lateral_taps, axis=2, keepdims=True)
    axial = axial_taps / jnp.sum(axial_taps, axis=1, keepdims=True)
    axial = jnp.pad(axial, ((0, 0), (0, 129)))
    wy = lateral[:, 1]
    gz, gy = lax.axis_index("gz"), lax.axis_index("gy")
    own = jnp.reshape(gz & 3, (1,))
    mask = jnp.reshape(32 * ((gz & 2) + (gy & 1)), (1,))

    packed = {}
    for k in ORDER:
        packed[k] = pack(after(own ^ k, *packed.values()), estimate)
    mine = {k: send(packed[k], to_block(k)) for k in ORDER}
    turned = {k: turn(after(own ^ k, *packed.values()), observed) for k in ORDER}
    seen = {2: send(turned[2], to_block(2)), 3: send(turned[3], to_block(3))}
    seen[0] = send(turned[0], to_block(0))
    seen[1] = send(turned[1], to_block(1))
    near = {2: send(after(mine[2], *turned.values()), to_next_z(2)), 0: send(after(mine[0], *turned.values()), to_next_z(0))}
    near[3] = send(after(mine[3], near[2]), to_next_z(3))
    near[1] = send(after(mine[1], near[0]), to_next_z(1))
    seen = [seen[k] for k in range(4)]
    z_taps, zt_taps, x_taps, xt_high, xt_low = weights(mask, lateral[:, 0], axial)

    pieces = [mine[k] for k in range(4)] + [near[k] for k in range(4)]
    blur_e, first, last = forward(edge_group, pieces, z_taps, x_taps, True)
    low, high = send(last, to_next_y(1)), send(first, to_next_y(-1))
    (blur_i,) = forward(inner_group, pieces, z_taps, x_taps, False)
    ratio_e, first, last = along_y(
        "ratio_e", EDGE_ROWS, False, wy, blur_e, blur_i, [low, high], seen
    )
    (ratio_i,) = along_y("ratio_i", INNER_ROWS, False, wy, blur_e, blur_i, [], seen)
    low, high = send(last, to_next_y(1)), send(first, to_next_y(-1))
    (back_i,) = along_y("back_i", INNER_ROWS, True, wy, ratio_e, ratio_i, [], [])
    parts_i = backward(back_i, xt_high, xt_low, zt_taps)
    (back_e,) = along_y("back_e", EDGE_ROWS, True, wy, ratio_e, ratio_i, [low, high], [])
    parts_e = backward(back_e, xt_high, xt_low, zt_taps)
    result = None
    for group, parts in ((inner_group, parts_i), (edge_group, parts_e)):
        outer = [send(parts[4 + pair], reverse(to_next_z(2 * pair))) for pair in range(2)]
        home = [
            send(parts[k] + outer[k // 2][k % 2], reverse(to_block(k))) for k in range(4)
        ]
        result = finish(group, own, home, estimate, result)
    return result


def solution(mesh):
    return jax.shard_map(
        on_device,
        mesh=mesh,
        in_specs=(P("gz", "gy", None), P(None, "gz", "gy", None), P(), P()),
        out_specs=P("gz", "gy", None),
        check_vma=False,
    )
```

```python
import jax
import jax.numpy as jnp
from jax import lax
from jax.experimental import pallas as pl
from jax.experimental.pallas import tpu as pltpu
from jax.sharding import PartitionSpec as P

AXES = ("gz", "gy")
F32 = jnp.float32
BF16 = jnp.bfloat16
VMEM_LIMIT = 24 * 1024 * 1024


def device(z, h, c, y, l):
    return ((z * 2 + h) * 2 + c) * 8 + y * 2 + l


def everyone():
    for z in range(4):
        for h in range(2):
            for c in range(2):
                for y in range(4):
                    for l in range(2):
                        yield z, h, c, y, l


def to_block(k):
    pairs = []
    for z, h, c, y, l in everyone():
        target = (2 * h + c) ^ k
        pairs.append((device(z, h, c, y, l), device(z, target >> 1, l, y, target & 1)))
    return pairs


def to_next_z(k):
    pairs = []
    for z, h, c, y, l in everyone():
        other = z - 1 if (h ^ (k >> 1)) == 0 else z + 1
        if 0 <= other < 4:
            pairs.append((device(z, h, c, y, l), device(other, h, c, y, l)))
    return pairs


def to_next_y(step):
    pairs = []
    for z, h, c, y, l in everyone():
        run = 2 * y + c + step
        if 0 <= run < 8:
            pairs.append((device(z, h, c, y, l), device(z, h, run & 1, run >> 1, l)))
    return pairs


def reverse(pairs):
    return [(target, source) for source, target in pairs]


def halves(value):
    high = value.astype(BF16)
    low = (value - high.astype(F32)).astype(BF16)
    return high, low


def mxu(left, right):
    return jnp.dot(left, right, preferred_element_type=F32)


def shape(dims, dtype=F32):
    return jax.ShapeDtypeStruct(dims, dtype)


def whole(dims):
    return pl.BlockSpec(dims, lambda *_: (0,) * len(dims))


SMEM = pl.BlockSpec(memory_space=pltpu.SMEM)
PIECE = (2, 9, 32, 128)
WHOLE_PIECE = (4, 9, 32, 128)
PIECE_BLOCK = pl.BlockSpec((1, 9, 32, 128), lambda g, *_: (g, 0, 0, 0))


def edge_group(g):
    return 3 * g


def inner_group(g):
    return g + 1


ORDER = (0, 2, 3, 1)
EDGE_ROWS = list(range(0, 8)) + list(range(24, 32))
INNER_ROWS = list(range(8, 24))


def params():
    return pltpu.CompilerParams(vmem_limit_bytes=VMEM_LIMIT)


def cost(flops, count):
    return pl.CostEstimate(flops=1024, bytes_accessed=1024, transcendentals=0)


def pack_kernel(column_ref, centre_ref, left_ref, right_ref, out_ref):
    column = column_ref[0]
    lane = lax.broadcasted_iota(jnp.int32, (32, 128), 1)
    take_left = jnp.logical_and(lane >= 120, column > 0)
    take_right = jnp.logical_and(lane < 8, column < 3)
    centre = centre_ref.reshape(256, 128)
    left = left_ref.reshape(256, 128)
    right = right_ref.reshape(256, 128)
    strips = jnp.zeros((32, 128), F32)
    for e in range(8):
        rows = pl.ds(e, 32, stride=8)
        out_ref[0, e] = centre[rows, :]
        edge = jnp.where(take_left, left[rows, :], jnp.where(take_right, right[rows, :], 0.0))
        strips = strips + pltpu.roll(edge, (16 * e + 8) % 128, 1)
    out_ref[0, 8] = strips


def pack(column, estimate):
    block = (32, 8, 128)
    return pl.pallas_call(
        pack_kernel,
        grid_spec=pltpu.PrefetchScalarGridSpec(
            num_scalar_prefetch=1,
            grid=(4,),
            in_specs=[
                pl.BlockSpec(block, lambda g, s: (0, g, s[0])),
                pl.BlockSpec(block, lambda g, s: (0, g, jnp.maximum(s[0] - 1, 0))),
                pl.BlockSpec(block, lambda g, s: (0, g, jnp.minimum(s[0] + 1, 3))),
            ],
            out_specs=PIECE_BLOCK,
        ),
        out_shape=shape(WHOLE_PIECE),
        compiler_params=params(),
        cost_estimate=cost(1 << 20, 12 << 20),
        name="pack",
    )(column, estimate, estimate, estimate)


def turn_kernel(column_ref, in_ref, out_ref):
    for v in range(2):
        rows = in_ref.at[v].reshape(256, 128)
        for e in range(8):
            out_ref[v, e] = rows[pl.ds(e, 32, stride=8), :]


def turn(column, observed):
    return pl.pallas_call(
        turn_kernel,
        grid_spec=pltpu.PrefetchScalarGridSpec(
            num_scalar_prefetch=1,
            grid=(4,),
            in_specs=[pl.BlockSpec((2, 32, 8, 128), lambda g, s: (0, 0, g, s[0]))],
            out_specs=pl.BlockSpec((2, 8, 32, 128), lambda g, s: (0, g, 0, 0)),
        ),
        out_shape=shape((2, 32, 32, 128)),
        compiler_params=params(),
        cost_estimate=cost(1 << 20, 6 << 20),
        name="turn",
    )(column, observed)


def weights_kernel(mask_ref, wx_ref, wz_ref, z_ref, zt_ref, x_ref, xth_ref, xtl_ref):
    mask = mask_ref[0]
    row = lax.broadcasted_iota(jnp.int32, (128, 256), 0) ^ mask
    lane = lax.broadcasted_iota(jnp.int32, (128, 256), 1)
    parts = []
    for v in range(2):
        band = jnp.broadcast_to(wz_ref[v : v + 1, :], (128, 256))
        band = pltpu.roll(band, 256 - 63, 1)
        for bit in range(7):
            step = 1 << bit
            band = jnp.where((row & step) != 0, pltpu.roll(band, step, 1), band)
        for step in (32, 64):
            other = jnp.where(
                (lane & step) == 0, pltpu.roll(band, 256 - step, 1), pltpu.roll(band, step, 1)
            )
            band = jnp.where(((lane * 0 + mask) & step) != 0, other, band)
        parts.append(band)
    full = jnp.concatenate(parts, axis=0)
    high, low = halves(full)
    z_ref[:, 0:256] = high
    z_ref[:, 256:512] = low
    z_ref[:, 512:768] = high
    high, low = halves(full.T)
    zt_ref[:, 0:256] = high
    zt_ref[:, 256:512] = low
    zt_ref[:, 512:768] = high

    def x_taps(dims, column_dim, v):
        spot = lax.broadcasted_iota(jnp.int32, dims, column_dim)
        own = lax.broadcasted_iota(jnp.int32, dims, 1 - column_dim)
        strip = spot & 15
        column = jnp.where(spot < 128, spot + 8, jnp.where(strip < 8, strip, strip + 128))
        tap = column - own - 1
        total = jnp.zeros(dims, F32)
        for t in range(15):
            total = jnp.where(tap == t, wx_ref[v, t], total)
        return spot, total

    for v in range(2):
        spot, total = x_taps((256, 128), 0, v)
        for e in range(8):
            keep = jnp.logical_or(spot < 128, (spot - 128) // 16 == e)
            high, low = halves(jnp.where(keep, total, 0.0))
            x_ref[v, e, :, 0:128] = high
            x_ref[v, e, :, 128:256] = low
        spot, total = x_taps((128, 256), 1, v)
        for e in range(8):
            keep = jnp.logical_or(spot < 128, (spot - 128) // 16 == e)
            high, low = halves(jnp.where(keep, total, 0.0))
            xth_ref[v, e] = high
            xtl_ref[v, e] = low


def weights(mask, wx, wz):
    outs = [
        shape((256, 768), BF16),
        shape((256, 768), BF16),
        shape((2, 8, 256, 256), BF16),
        shape((2, 8, 128, 256), BF16),
        shape((2, 8, 128, 256), BF16),
    ]
    return pl.pallas_call(
        weights_kernel,
        in_specs=[SMEM, SMEM, pl.BlockSpec(memory_space=pltpu.VMEM)],
        out_specs=[pl.BlockSpec(memory_space=pltpu.VMEM)] * 5,
        out_shape=outs,
        compiler_params=params(),
        cost_estimate=cost(1 << 24, 16 << 20),
        name="weights",
    )(mask, wx, wz)


def forward_kernel(*refs):
    pieces = refs[:8]
    z_ref, x_ref, out_ref = refs[8:11]
    z_taps = z_ref[...]

    def along_z(rows):
        lines = [jnp.concatenate([ref[0, row] for ref in pieces], axis=0) for row in rows]
        field = jnp.concatenate(lines, axis=1) if len(lines) > 1 else lines[0]
        high, low = halves(field)
        return mxu(z_taps, jnp.concatenate([high, high, low], axis=0))

    strips = along_z([8])
    strip_halves = [halves(strips[128 * v : 128 * v + 128]) for v in range(2)]
    for pair in range(4):
        both = along_z([2 * pair, 2 * pair + 1])
        for at in range(2):
            e = 2 * pair + at
            for v in range(2):
                high, low = halves(both[128 * v : 128 * v + 128, 128 * at : 128 * at + 128])
                high = jnp.concatenate([high, strip_halves[v][0]], axis=1)
                low = jnp.concatenate([low, strip_halves[v][1]], axis=1)
                first = mxu(high, x_ref[v, e])
                second = mxu(low, x_ref[v, e, :, 0:128])
                out_ref[v, e] = (first[:, 0:128] + first[:, 128:256]) + second
    if len(refs) > 11:
        first_ref, last_ref = refs[11:]

        @pl.when(pl.program_id(0) == 0)
        def _():
            first_ref[...] = out_ref[:, 0:7]

        @pl.when(pl.program_id(0) == 1)
        def _():
            last_ref[...] = out_ref[:, 1:8]


def forward(group, pieces, z_taps, x_taps, edges):
    out_specs = [pl.BlockSpec((2, 8, 128, 128), lambda g: (0, g, 0, 0))]
    out_shape = [shape((2, 16, 128, 128))]
    if edges:
        out_specs += [whole((2, 7, 128, 128))] * 2
        out_shape += [shape((2, 7, 128, 128))] * 2
    return pl.pallas_call(
        forward_kernel,
        grid=(2,),
        in_specs=[pl.BlockSpec((1, 9, 32, 128), lambda g: (group(g), 0, 0, 0))] * 8
        + [whole((256, 768)), whole((2, 8, 256, 256))],
        out_specs=out_specs,
        out_shape=out_shape,
        compiler_params=params(),
        cost_estimate=cost(4 << 30, 12 << 20),
        name="forward",
    )(*pieces, z_taps, x_taps)


def y_kernel(rows, flip, with_edges, with_ratio):
    def kernel(wy_ref, edge_ref, inner_ref, *refs):
        refs = list(refs)
        low_ref, high_ref = (refs.pop(0), refs.pop(0)) if with_edges else (None, None)
        observed = [refs.pop(0) for _ in range(4)] if with_ratio else []
        out_ref = refs.pop(0)
        v = pl.program_id(0)
        taps = [wy_ref[v, 14 - t if flip else t] for t in range(15)]

        def sums(start, store):
            def line(row):
                part = pl.ds(start, 8)
                if row < 0:
                    return low_ref[0, row + 7, part, :]
                if row < 8:
                    return edge_ref[0, row, part, :]
                if row < 24:
                    return inner_ref[0, row - 8, part, :]
                if row < 32:
                    return edge_ref[0, row - 16, part, :]
                return high_ref[0, row - 32, part, :]

            for at, row in enumerate(rows):
                total = taps[0] * line(row - 7)
                for t in range(1, 15):
                    total = total + taps[t] * line(row + t - 7)
                store(at, row, total)

        if not with_ratio:

            @pl.loop(0, 16)
            def _(part):
                start = pl.multiple_of(part * 8, 8)

                def store(at, row, total):
                    out_ref[0, at, pl.ds(start, 8), :] = total

                sums(start, store)

            return

        for k in range(4):

            @pl.loop(0, 4)
            def _(part, k=k):
                inner = pl.multiple_of(part * 8, 8)
                start = pl.multiple_of(32 * k + part * 8, 8)

                def store(at, row, total):
                    ratio = observed[k][0, row, pl.ds(inner, 8), :] / total
                    out_ref[0, at, pl.ds(start, 8), :] = ratio
                    if with_edges and row < 7:
                        refs[0][0, row, pl.ds(start, 8), :] = ratio
                    if with_edges and row > 24:
                        refs[1][0, row - 25, pl.ds(start, 8), :] = ratio

                sums(start, store)

    return kernel


def along_y(name, rows, flip, wy, edge, inner, outer, observed):
    seven = pl.BlockSpec((1, 7, 128, 128), lambda v: (v, 0, 0, 0))
    chunk = pl.BlockSpec((1, 16, 128, 128), lambda v: (v, 0, 0, 0))
    quarter = pl.BlockSpec((1, 32, 32, 128), lambda v: (v, 0, 0, 0))
    gives_edges = len(outer) > 0 and len(observed) > 0
    return pl.pallas_call(
        y_kernel(rows, flip, len(outer) > 0, len(observed) > 0),
        grid=(2,),
        in_specs=[SMEM, chunk, chunk] + [seven] * len(outer) + [quarter] * len(observed),
        out_specs=[chunk] + [seven] * (2 * gives_edges),
        out_shape=[shape((2, 16, 128, 128))] + [shape((2, 7, 128, 128))] * (2 * gives_edges),
        compiler_params=params(),
        cost_estimate=cost(15 << 20, 12 << 20),
        name=name,
    )(wy, edge, inner, *outer, *observed)


def backward_kernel(in_ref, xth_ref, xtl_ref, zt_ref, *outs):
    zt_taps = zt_ref[...]

    def along_z(fields, rows):
        high, low = halves(jnp.concatenate(fields, axis=1) if len(fields) > 1 else fields[0])
        result = mxu(zt_taps, jnp.concatenate([high, high, low], axis=0))
        for at, row in enumerate(rows):
            for m in range(8):
                part = result[32 * m : 32 * m + 32, 128 * at : 128 * at + 128]
                if m < 4:
                    outs[m][0, row] = part
                else:
                    outs[4 + (m - 4) // 2][m % 2, 0, row] = part

    strips = [jnp.zeros((128, 128), F32), jnp.zeros((128, 128), F32)]
    for pair in range(4):
        fields = []
        for e in (2 * pair, 2 * pair + 1):
            mains = []
            for v in range(2):
                high, low = halves(in_ref[v, e])
                right = xth_ref[v, e]
                wide = mxu(
                    jnp.concatenate([high, low], axis=1), jnp.concatenate([right, right], axis=0)
                ) + mxu(high, xtl_ref[v, e])
                mains.append(wide[:, 0:128])
                strips[v] = strips[v] + wide[:, 128:256]
            fields.append(jnp.concatenate(mains, axis=0))
        along_z(fields, [2 * pair, 2 * pair + 1])
    along_z([jnp.concatenate(strips, axis=0)], [8])


def backward(field, xt_high, xt_low, zt_taps):
    return pl.pallas_call(
        backward_kernel,
        grid=(2,),
        in_specs=[
            pl.BlockSpec((2, 8, 128, 128), lambda g: (0, g, 0, 0)),
            whole((2, 8, 128, 256)),
            whole((2, 8, 128, 256)),
            whole((256, 768)),
        ],
        out_specs=[PIECE_BLOCK] * 4
        + [pl.BlockSpec((2, 1, 9, 32, 128), lambda g: (0, g, 0, 0, 0))] * 2,
        out_shape=[shape(PIECE)] * 4 + [shape((2,) + PIECE)] * 2,
        compiler_params=params(),
        cost_estimate=cost(4 << 30, 12 << 20),
        name="backward",
    )(field, xt_high, xt_low, zt_taps)


def finish_kernel(own_ref, p0, p1, p2, p3, estimate_ref, *refs):
    out_ref, all_ref, turn_ref = refs[-3:]
    own = own_ref[0]
    for k, ref in enumerate((p0, p1, p2, p3)):
        all_ref[own ^ k] = ref[0]
    lane = lax.broadcasted_iota(jnp.int32, (32, 128), 1)
    ends = jnp.logical_or(lane >= 120, lane < 8)
    from_next = (lane & 8) == 0
    for j in range(4):
        zero = jnp.zeros((32, 128), F32)
        after = all_ref[j + 1, 8] if j < 3 else zero
        before = all_ref[j - 1, 8] if j > 0 else zero
        strips = jnp.where(from_next, after, before)
        for e in range(8):
            moved = pltpu.roll(strips, (120 - 16 * e) % 128, 1)
            turn_ref[pl.ds(e, 32, stride=8), :] = all_ref[j, e] + jnp.where(ends, moved, 0.0)
        columns = pl.ds(128 * j, 128)
        total = turn_ref[...].reshape(32, 8, 128)
        out_ref[:, :, columns] = estimate_ref[:, :, columns] * (0.5 * total)


def finish(group, own, pieces, estimate, partial):
    slab = pl.BlockSpec((32, 8, 512), lambda g, s: (0, group(g), 0))
    more = [] if partial is None else [partial]
    return pl.pallas_call(
        finish_kernel,
        grid_spec=pltpu.PrefetchScalarGridSpec(
            num_scalar_prefetch=1,
            grid=(2,),
            in_specs=[PIECE_BLOCK] * 4 + [slab] + [pl.BlockSpec(memory_space=pl.ANY)] * len(more),
            out_specs=slab,
            scratch_shapes=[pltpu.VMEM((4, 9, 32, 128), F32), pltpu.VMEM((256, 128), F32)],
        ),
        out_shape=shape((32, 32, 512)),
        input_output_aliases={6: 0} if more else {},
        compiler_params=params(),
        cost_estimate=cost(2 << 20, 6 << 20),
        name="finish",
    )(own, *pieces, estimate, *more)


def send(value, pairs):
    return lax.ppermute(value, AXES, pairs)


def after(value, *others):
    return lax.optimization_barrier((value, *others))[0]


def on_device(estimate, observed, lateral_taps, axial_taps):
    lateral = lateral_taps / jnp.sum(lateral_taps, axis=2, keepdims=True)
    axial = axial_taps / jnp.sum(axial_taps, axis=1, keepdims=True)
    axial = jnp.pad(axial, ((0, 0), (0, 129)))
    wy = lateral[:, 1]
    gz, gy = lax.axis_index("gz"), lax.axis_index("gy")
    own = jnp.reshape(gz & 3, (1,))
    mask = jnp.reshape(32 * ((gz & 2) + (gy & 1)), (1,))

    packed = {}
    for k in ORDER:
        packed[k] = pack(after(own ^ k, *packed.values()), estimate)
    mine = {k: send(packed[k], to_block(k)) for k in ORDER}
    turned = {k: turn(after(own ^ k, *packed.values()), observed) for k in ORDER}
    seen = {2: send(turned[2], to_block(2)), 3: send(turned[3], to_block(3))}
    seen[0] = send(turned[0], to_block(0))
    seen[1] = send(turned[1], to_block(1))
    near = {2: send(after(mine[2], *turned.values()), to_next_z(2)), 0: send(after(mine[0], *turned.values()), to_next_z(0))}
    near[3] = send(after(mine[3], near[2]), to_next_z(3))
    near[1] = send(after(mine[1], near[0]), to_next_z(1))
    seen = [seen[k] for k in range(4)]
    z_taps, zt_taps, x_taps, xt_high, xt_low = weights(mask, lateral[:, 0], axial)

    pieces = [mine[k] for k in range(4)] + [near[k] for k in range(4)]
    blur_e, first, last = forward(edge_group, pieces, z_taps, x_taps, True)
    low, high = send(last, to_next_y(1)), send(first, to_next_y(-1))
    (blur_i,) = forward(inner_group, pieces, z_taps, x_taps, False)
    ratio_e, first, last = along_y(
        "ratio_e", EDGE_ROWS, False, wy, blur_e, blur_i, [low, high], seen
    )
    (ratio_i,) = along_y("ratio_i", INNER_ROWS, False, wy, blur_e, blur_i, [], seen)
    low, high = send(last, to_next_y(1)), send(first, to_next_y(-1))
    (back_i,) = along_y("back_i", INNER_ROWS, True, wy, ratio_e, ratio_i, [], [])
    parts_i = backward(back_i, xt_high, xt_low, zt_taps)
    (back_e,) = along_y("back_e", EDGE_ROWS, True, wy, ratio_e, ratio_i, [low, high], [])
    parts_e = backward(back_e, xt_high, xt_low, zt_taps)
    result = None
    for group, parts in ((inner_group, parts_i), (edge_group, parts_e)):
        outer = [send(parts[4 + pair], reverse(to_next_z(2 * pair))) for pair in range(2)]
        home = [
            send(parts[k] + outer[k // 2][k % 2], reverse(to_block(k))) for k in range(4)
        ]
        result = finish(group, own, home, estimate, result)
    return result


def solution(mesh):
    return jax.shard_map(
        on_device,
        mesh=mesh,
        in_specs=(P("gz", "gy", None), P(None, "gz", "gy", None), P(), P()),
        out_specs=P("gz", "gy", None),
        check_vma=False,
    )
```
